32 devices in a mesh: leaf: 16 (over z, y, x), head: 2 (over core).
Axes of the slice: x: 2, y: 2, z: 4, core: 2. Of those that a mesh axis runs over, the one named last changes fastest.
Arguments:
- queries: bfloat16 [2048, 16, 576], P('leaf', 'head'), may hold values from -40 to 40
- leaf_latent: bfloat16 [2048, 576], P('leaf'), may hold values from -4 to 4
- node_latent: bfloat16 [16, 96, 576], P('leaf', 'head'), may hold values from -4 to 4
- grad_out: bfloat16 [2048, 16, 512], P('leaf', 'head'), may hold values from -6 to 6
- leaf_nodes: int32 [32, 3], P('leaf'), may hold values from 0 to 15, as said below
- leaf_lengths: int32 [32], P('leaf'), may hold values from 1 to 64, 1280 in all
Outputs:
- attention: bfloat16 [2048, 16, 512], P('leaf', 'head')
- node_grad: bfloat16 [16, 96, 576], P('leaf', 'head')
- leaf_grad: bfloat16 [2048, 576], P('leaf')
The draws below stay inside these ranges and needn't reach their ends.
Inputs may be any that keep to these rules, and one draw needn't show every extreme that they name: `leaf_nodes`: each row lists three different nodes: a root, one of its children and one of that child's children. Every node has one level and one parent; which nodes are used and how often varies.
All inputs are finite; a program needn't handle non-finite values. No bound on the sum of `leaf_lengths` on one device may be relied on, other than what follows from the above.
Results may differ from the reference program's by a relative error of at most 0.0095.
Values may be sent and summed in bfloat16 or wider, within the bound.
No kernel may reach another device: no remote copies, remote signals or barrier semaphores. Data moves between devices by JAX's collectives and lax.ppermute only.
A program may use at most 64 MiB of HBM per device.

```python
import math
import jax
import jax.numpy as jnp
import numpy as np
from jax import lax

LAT = 512
LEAF_ROWS = 64
NODE_ROWS = 96
LATW = 576
HEADS = 16
LEAVES = 32
ROWS = 2048
NODES = 16
KEYS = 352


def leaf_pair(key):
    base = jax.random.fold_in(key, 4242)
    key_lat, key_query = jax.random.split(base, 2)
    latent = jnp.clip(jax.random.normal(key_lat, (ROWS, LATW), jnp.float32), -4.0, 4.0).astype(jnp.bfloat16)
    query = jnp.clip(jax.random.normal(key_query, (ROWS, HEADS, LATW), jnp.float32), -6.0, 6.0)
    return (query.astype(jnp.bfloat16), latent)


def draw_queries(key, part):
    return leaf_pair(key)[0]


def draw_leaf_latent(key, part):
    return leaf_pair(key)[1]


def draw_leaf_nodes(key, part):
    base = jax.random.fold_in(key, 31)
    key_order, key_first, key_second = jax.random.split(base, 3)
    roots = max(NODES // 16, 1)
    middle = NODES * 3 // 16
    deepest = NODES - roots - middle
    order = jax.random.permutation(key_order, NODES)
    picked = jnp.minimum(jax.random.randint(key_first, (LEAVES,), 0, deepest), jax.random.randint(key_second, (LEAVES,), 0, deepest))
    middle_of = picked % middle
    root_of = middle_of % roots
    return jnp.stack([order[root_of], order[roots + middle_of], order[roots + middle + picked]], axis=1).astype(jnp.int32)


def shard_levels(key, shape, cuts, low, largest):
    def one(dim, blocks):
        heights = jax.random.uniform(jax.random.fold_in(jax.random.fold_in(key, 6), dim), (blocks,), jnp.float32, low / len(cuts), largest / len(cuts))
        return jnp.repeat(jnp.exp(heights), shape[dim] // blocks).reshape((-1,) + (1,) * (len(shape) - dim - 1))

    gain = one(*cuts[0])
    for cut in cuts[1:]:
        gain = gain * one(*cut)
    return gain


def profile(number_of, total, bound, lean):
    portions = [(1 << 20) // math.isqrt(standing ** lean) + 1 for standing in range(2, number_of + 1)]
    rest, given = total - bound - (number_of - 1), [1] * (number_of - 1)
    while rest > 0:
        movable = [i for i in range(number_of - 1) if given[i] < bound]
        mass, left = sum([portions[i] for i in movable]), rest
        for i in movable:
            addition = min(bound - given[i], max(1, left * portions[i] // mass), rest)
            given[i] = given[i] + addition
            rest = rest - addition
    return np.array([bound] + given)


def uneven(own_key, number_of, total, most, lean):
    if number_of == 2:
        one = jax.random.randint(own_key, (), max(1, total - most), min(most, total - 1) + 1)
        return jnp.stack([one, total - one])
    lengths = jnp.asarray(profile(number_of, total, most, lean), jnp.int32)
    pairs = (number_of - 1) // 2
    donor, sink = lengths[1:1 + 2 * pairs:2], lengths[2:2 + 2 * pairs:2]
    margin = jnp.minimum(donor - 1, most - sink)
    moved = jax.random.randint(jax.random.fold_in(own_key, 1), (pairs,), 0, 1 << 20) % (margin + 1)
    lengths = lengths.at[1:1 + 2 * pairs:2].set(donor - moved).at[2:2 + 2 * pairs:2].set(sink + moved)
    return lengths[jax.random.permutation(jax.random.fold_in(own_key, 2), number_of)]


def scatter_about(stream_key, shape, spread, bound, shards=(), kind=jnp.bfloat16):
    gain = shard_levels(stream_key, shape, shards, -0.22, 0.18) if shards else 1.0
    result = jax.random.normal(stream_key, shape, jnp.float32) * spread * gain
    return jnp.minimum(jnp.maximum(result, -bound), bound).astype(kind)


def setup_inputs(seed: int = 0) -> dict:
    splits = jax.random.split(jax.random.key(seed), 7)
    queries = draw_queries(jax.random.fold_in(splits[6], 71), 0)
    leaf_latent = draw_leaf_latent(jax.random.fold_in(splits[6], 71), 0)
    node_latent = scatter_about(splits[2], (NODES, NODE_ROWS, LATW), 1.0, 4.0, ((0, 16), (1, 2)))
    grad_out = scatter_about(splits[3], (ROWS, HEADS, LAT), 1.0, 6.0, ((0, 16), (1, 2)))
    leaf_nodes = draw_leaf_nodes(jax.random.fold_in(splits[6], 71), 0)
    leaf_lengths = uneven(splits[5], LEAVES, LEAVES * LEAF_ROWS * 5 // 8, LEAF_ROWS, 2).astype(jnp.int32)
    return dict(queries=queries, leaf_latent=leaf_latent, node_latent=node_latent, grad_out=grad_out, leaf_nodes=leaf_nodes, leaf_lengths=leaf_lengths)


score_scale = 192.0 ** -0.5


def reference(queries, leaf_latent, node_latent, grad_out, leaf_nodes, leaf_lengths):
    q_all = queries.reshape(LEAVES, LEAF_ROWS, HEADS, LATW)
    lat_all = leaf_latent.reshape(LEAVES, LEAF_ROWS, LATW)
    dout_all = grad_out.reshape(LEAVES, LEAF_ROWS, HEADS, LAT)
    row_index = jnp.arange(LEAF_ROWS, dtype=jnp.int32)
    key_index = jnp.arange(KEYS, dtype=jnp.int32)
    visible = (key_index[None, :] < 3 * NODE_ROWS) | ((key_index[None, :] - 3 * NODE_ROWS) <= row_index[:, None])

    def one_leaf(accum, items):
        query, own, dout, ids, length = items
        keys = jnp.concatenate([node_latent[ids].reshape(3 * NODE_ROWS, LATW), own], axis=0)
        live = (row_index < length).astype(jnp.float32)
        keys_f = keys.astype(jnp.float32)
        values_f = keys_f[:, :LAT]
        query_f = query.astype(jnp.float32)
        scores = jnp.einsum('rhc,kc->rhk', query_f, keys_f) * score_scale
        scores = jnp.where(visible[:, None, :], scores, -jnp.inf)
        top = jnp.max(scores, axis=-1, keepdims=True)
        expo = jnp.exp(scores - top)
        probs = expo / jnp.sum(expo, axis=-1, keepdims=True)
        probs_b = probs.astype(jnp.bfloat16).astype(jnp.float32)
        outputs = jnp.einsum('rhk,kc->rhc', probs_b, values_f)
        attn = (outputs * live[:, None, None]).astype(jnp.bfloat16)
        masked = (dout.astype(jnp.float32) * live[:, None, None]).astype(jnp.bfloat16).astype(jnp.float32)
        dprobs = jnp.einsum('rhc,kc->rhk', masked, values_f)
        delta = jnp.sum(masked * outputs, axis=-1)
        dscores = (score_scale * probs * (dprobs - delta[..., None])).astype(jnp.bfloat16).astype(jnp.float32)
        grad_keys = jnp.einsum('rhk,rhc->kc', dscores, query_f)
        grad_values = jnp.einsum('rhk,rhc->kc', probs_b, masked)
        grad_keys = jnp.concatenate([grad_keys[:, :LAT] + grad_values, grad_keys[:, LAT:]], axis=1)
        accum = accum.at[ids].add(grad_keys[:3 * NODE_ROWS].reshape(3, NODE_ROWS, LATW))
        return accum, (attn, grad_keys[3 * NODE_ROWS:].astype(jnp.bfloat16))

    start = jnp.zeros((NODES, NODE_ROWS, LATW), jnp.float32)
    accum, (attn, own_grad) = lax.scan(one_leaf, start, (q_all, lat_all, dout_all, leaf_nodes.astype(jnp.int32), leaf_lengths.astype(jnp.int32)))
    return attn.reshape(ROWS, HEADS, LAT), accum.astype(jnp.bfloat16), own_grad.reshape(ROWS, LATW)
```

```python
import functools

import jax
import jax.numpy as jnp
from jax import lax
from jax.experimental import pallas as pl
from jax.experimental.pallas import tpu as pltpu
from jax.sharding import PartitionSpec as P

LAT = 512
LEVELS = 3

score_scale = 192.0 ** (-0.5)

NT = (((1,), (1,)), ((), ()))
NN = (((1,), (0,)), ((), ()))
TN = (((0,), (0,)), ((), ()))


def dot(a, b, dims):
    return lax.dot_general(a, b, dims, preferred_element_type=jnp.float32)


def vmem(count):
    return [pl.BlockSpec(memory_space=pltpu.VMEM)] * count


def cost(flops, moved):
    return pl.CostEstimate(flops=flops, bytes_accessed=moved, transcendentals=0)


def select_kernel(where_ref, table_ref, out_ref):
    for slot in range(out_ref.shape[0]):
        out_ref[slot] = table_ref[where_ref[slot]]


def select(where, table):
    slots = where.shape[0]
    shape = (slots,) + table.shape[1:]
    return pl.pallas_call(
        select_kernel,
        out_shape=jax.ShapeDtypeStruct(shape, table.dtype),
        in_specs=[pl.BlockSpec(memory_space=pltpu.SMEM)] + vmem(1),
        out_specs=vmem(1)[0],
        name="select_nodes",
    )(where, table)


def grads_kernel(parts, leaves, heads, len_ref, own_ref, query_ref, grad_ref, *refs):
    part_refs, refs = refs[:parts], refs[parts:]
    term_refs, refs = refs[:parts], refs[parts:]
    own_grad_ref, probs_ref, keys_ref, key_ref, dscore_ref = refs
    slice_rows, width = part_refs[0].shape[1:]
    leaf_rows = own_ref.shape[0] // leaves
    lines = leaf_rows * heads
    node_rows = LEVELS * parts * slice_rows
    total_keys = node_rows + leaf_rows
    for leaf in range(leaves):
        for part in range(parts):
            for level in range(LEVELS):
                row = (part * LEVELS + level) * slice_rows
                key_ref[row : row + slice_rows, :] = part_refs[part][leaf * LEVELS + level]
        key_ref[node_rows:, :] = own_ref[leaf * leaf_rows : (leaf + 1) * leaf_rows, :]
        keys = key_ref[...]
        keys_ref[leaf] = keys
        query = query_ref[leaf * lines : (leaf + 1) * lines, :]
        grad = grad_ref[leaf * lines : (leaf + 1) * lines, :]
        scores = dot(keys, query, NT) * score_scale
        row_of = lax.broadcasted_iota(jnp.int32, (leaf_rows, lines), 1) // heads
        own_key = lax.broadcasted_iota(jnp.int32, (leaf_rows, lines), 0)
        own_scores = jnp.where(own_key <= row_of, scores[node_rows:], -jnp.inf)
        scores = jnp.concatenate([scores[:node_rows], own_scores], axis=0)
        top = jnp.max(scores, axis=0, keepdims=True)
        expo = jnp.exp(scores - top)
        live = lax.broadcasted_iota(jnp.int32, (1, lines), 1) // heads < len_ref[leaf]
        scale = jnp.where(live, 1.0, 0.0) / jnp.sum(expo, axis=0, keepdims=True)
        probs = expo * scale
        probs_b = probs.astype(jnp.bfloat16)
        probs_ref[leaf] = probs_b
        dprobs = dot(keys[:, :LAT], grad, NT)
        delta = jnp.sum(probs_b.astype(jnp.float32) * dprobs, axis=0, keepdims=True)
        dscore_ref[...] = (score_scale * probs * (dprobs - delta)).astype(jnp.bfloat16)
        dscores = dscore_ref[...]
        head_part = dot(dscores, query[:, :LAT], NN) + dot(probs_ref[leaf], grad, NN)
        tail_part = dot(dscores, query[:, LAT:], NN)
        for part in range(parts):
            for level in range(LEVELS):
                row = (part * LEVELS + level) * slice_rows
                ref = term_refs[part]
                ref[leaf * LEVELS + level, :, :LAT] = head_part[row : row + slice_rows].astype(ref.dtype)
                ref[leaf * LEVELS + level, :, LAT:] = tail_part[row : row + slice_rows].astype(ref.dtype)
        first = leaf * leaf_rows
        own_grad_ref[first : first + leaf_rows, :LAT] = head_part[node_rows:].astype(jnp.bfloat16)
        own_grad_ref[first : first + leaf_rows, LAT:] = tail_part[node_rows:].astype(jnp.bfloat16)


def grads(lengths, own, query, grad, parts, leaves, heads):
    slots, slice_rows, width = parts[0].shape
    rows = own.shape[0]
    lines = rows * heads // leaves
    total_keys = LEVELS * len(parts) * slice_rows + rows // leaves
    outs = [
        jax.ShapeDtypeStruct((slots, slice_rows, width), jnp.float32 if i == 0 else jnp.bfloat16)
        for i in range(len(parts))
    ] + [
        jax.ShapeDtypeStruct((rows, width), jnp.bfloat16),
        jax.ShapeDtypeStruct((leaves, total_keys, lines), jnp.bfloat16),
        jax.ShapeDtypeStruct((leaves, total_keys, width), jnp.bfloat16),
    ]
    return pl.pallas_call(
        functools.partial(grads_kernel, len(parts), leaves, heads),
        out_shape=outs,
        in_specs=[pl.BlockSpec(memory_space=pltpu.SMEM)] + vmem(3 + len(parts)),
        out_specs=vmem(len(outs)),
        scratch_shapes=[
            pltpu.VMEM((total_keys, width), jnp.bfloat16),
            pltpu.VMEM((total_keys, lines), jnp.bfloat16),
        ],
        compiler_params=pltpu.CompilerParams(vmem_limit_bytes=40 << 20),
        cost_estimate=cost(2 * rows * heads * total_keys * 4 * width, 8 << 20),
        name="attend_grads",
    )(lengths, own, query, grad, *parts)


def outputs_kernel(leaves, probs_ref, keys_ref, out_ref):
    lines = probs_ref.shape[2]
    for leaf in range(leaves):
        out = dot(probs_ref[leaf], keys_ref[leaf, :, :LAT], TN)
        out_ref[leaf * lines : (leaf + 1) * lines, :] = out.astype(jnp.bfloat16)


def outputs(probs, keys):
    leaves, total_keys, lines = probs.shape
    return pl.pallas_call(
        functools.partial(outputs_kernel, leaves),
        out_shape=jax.ShapeDtypeStruct((leaves * lines, LAT), jnp.bfloat16),
        in_specs=vmem(2),
        out_specs=vmem(1)[0],
        compiler_params=pltpu.CompilerParams(vmem_limit_bytes=24 << 20),
        cost_estimate=cost(2 * leaves * total_keys * lines * LAT, 4 << 20),
        name="attend_outputs",
    )(probs, keys)


def spread_kernel(shares, where_ref, *refs):
    share_refs, rest = refs[:shares], refs[shares:]
    keep_ref, send_refs, table_ref = rest[0], rest[1:-1], rest[-1]
    inner = keep_ref.shape[0]
    table_ref[...] = jnp.zeros_like(table_ref)
    for slot in range(share_refs[0].shape[0]):
        total = share_refs[0][slot]
        for ref in share_refs[1:]:
            total = total + ref[slot].astype(jnp.float32)
        table_ref[where_ref[slot]] += total
    keep_ref[...] = table_ref[:inner]
    for i, ref in enumerate(send_refs):
        ref[...] = table_ref[(i + 1) * inner : (i + 2) * inner].astype(jnp.bfloat16)


def spread(where, shares, outer, inner):
    block = shares[0].shape[1:]
    outs = [jax.ShapeDtypeStruct((inner,) + block, jnp.float32)] + [
        jax.ShapeDtypeStruct((inner,) + block, jnp.bfloat16)
    ] * (outer - 1)
    return pl.pallas_call(
        functools.partial(spread_kernel, len(shares)),
        out_shape=outs,
        in_specs=[pl.BlockSpec(memory_space=pltpu.SMEM)] + vmem(len(shares)),
        out_specs=vmem(len(outs)),
        scratch_shapes=[pltpu.VMEM((outer * inner,) + block, jnp.float32)],
        compiler_params=pltpu.CompilerParams(vmem_limit_bytes=40 << 20),
        name="spread_terms",
    )(where, *shares)


def merge_kernel(count, *refs):
    keep_ref, got_refs, out_refs = refs[0], refs[1:count], refs[count:]
    for i, ref in enumerate(out_refs):
        total = keep_ref[i]
        for got in got_refs:
            total = total + got[i].astype(jnp.float32)
        ref[0] = total.astype(ref.dtype)


def merge(keep, got):
    inner = keep.shape[0]
    block = (1,) + keep.shape[1:]
    outs = [jax.ShapeDtypeStruct(block, jnp.float32)] + [
        jax.ShapeDtypeStruct(block, jnp.bfloat16)
    ] * (inner - 1)
    return pl.pallas_call(
        functools.partial(merge_kernel, 1 + len(got)),
        out_shape=outs,
        in_specs=vmem(1 + len(got)),
        out_specs=vmem(len(outs)),
        compiler_params=pltpu.CompilerParams(vmem_limit_bytes=40 << 20),
        name="merge_terms",
    )(keep, *got)


def body(leaf_size, head_size, queries, leaf_latent, node_latent, grad_out, leaf_nodes, leaf_lengths):
    rows, heads, width = queries.shape
    leaves = leaf_nodes.shape[0]
    side = 1
    while side * side < leaf_size:
        side *= 2
    axes = ("leaf", "head")

    def step(value, which, distance):
        pairs = []
        for leaf in range(leaf_size):
            for head in range(head_size):
                far = (which + head) % 2 == 0
                target = leaf ^ (distance * side if far else distance)
                pairs.append((leaf * head_size + head, target * head_size + head))
        return lax.ppermute(value, axes, pairs)

    def swap(value, distance):
        return lax.ppermute(value, "head", [(i, i ^ distance) for i in range(head_size)])

    relative = leaf_nodes.reshape(-1) ^ lax.axis_index("leaf")
    far, near = relative // side, relative % side
    even = lax.axis_index("head") % 2 == 0
    where = jnp.where(even, near * side + far, far * side + near)

    inner = jnp.concatenate([node_latent] + [step(node_latent, 0, d) for d in range(1, side)], axis=0)
    table = jnp.concatenate([inner] + [step(inner, 1, d) for d in range(1, side)], axis=0)
    mine = select(where, table)
    parts = [mine] + [swap(mine, d) for d in range(1, head_size)]

    query = queries.reshape(rows * heads, width)
    grad = grad_out.reshape(rows * heads, LAT)
    results = grads(leaf_lengths, leaf_latent, query, grad, parts, leaves, heads)
    terms, (own_grad, probs, keys) = results[:head_size], results[head_size:]

    shares = [terms[0]] + [swap(terms[d], d) for d in range(1, head_size)]
    keep, *sends = spread(where, shares, side, side)
    got = [step(send, 1, d + 1) for d, send in enumerate(sends)]
    attention = outputs(probs, keys).reshape(rows, heads, LAT)
    keep, *sends = merge(keep, got)
    total = keep
    for d, send in enumerate(sends):
        total = total + step(send, 0, d + 1).astype(jnp.float32)
    node_grad = total.astype(jnp.bfloat16)

    leaf_grad = own_grad
    distance = 1
    while distance < head_size:
        leaf_grad = leaf_grad + swap(leaf_grad, distance)
        distance *= 2
    return (attention, node_grad, leaf_grad)


def solution(mesh):
    return jax.shard_map(
        functools.partial(body, mesh.shape["leaf"], mesh.shape["head"]),
        mesh=mesh,
        in_specs=(
            P("leaf", "head", None),
            P("leaf", None),
            P("leaf", "head", None),
            P("leaf", "head", None),
            P("leaf", None),
            P("leaf"),
        ),
        out_specs=(P("leaf", "head", None), P("leaf", "head", None), P("leaf", None)),
        check_vma=False,
    )
```

```python
import functools

import jax
import jax.numpy as jnp
from jax import lax
from jax.experimental import pallas as pl
from jax.experimental.pallas import tpu as pltpu
from jax.sharding import PartitionSpec as P

LAT = 512
LEVELS = 3

score_scale = 192.0 ** (-0.5)

NT = (((1,), (1,)), ((), ()))
NN = (((1,), (0,)), ((), ()))
TN = (((0,), (0,)), ((), ()))


def dot(a, b, dims):
    return lax.dot_general(a, b, dims, preferred_element_type=jnp.float32)


def vmem(count):
    return [pl.BlockSpec(memory_space=pltpu.VMEM)] * count


def cost(flops, moved):
    return pl.CostEstimate(flops=flops, bytes_accessed=moved, transcendentals=0)


def select_kernel(where_ref, table_ref, out_ref):
    for slot in range(out_ref.shape[0]):
        out_ref[slot] = table_ref[where_ref[slot]]


def select(where, table):
    slots = where.shape[0]
    shape = (slots,) + table.shape[1:]
    return pl.pallas_call(
        select_kernel,
        out_shape=jax.ShapeDtypeStruct(shape, table.dtype),
        in_specs=[pl.BlockSpec(memory_space=pltpu.SMEM)] + vmem(1),
        out_specs=vmem(1)[0],
        compiler_params=pltpu.CompilerParams(vmem_limit_bytes=4 << 20),
        name="select_nodes",
    )(where, table)


def grads_kernel(parts, leaves, heads, len_ref, own_ref, query_ref, grad_ref, *refs):
    part_refs, refs = refs[:parts], refs[parts:]
    term_refs, refs = refs[:parts], refs[parts:]
    own_grad_ref, probs_ref, keys_ref, key_ref, dscore_ref = refs
    slice_rows, width = part_refs[0].shape[1:]
    leaf_rows = own_ref.shape[0] // leaves
    lines = leaf_rows * heads
    node_rows = LEVELS * parts * slice_rows
    total_keys = node_rows + leaf_rows
    for leaf in range(leaves):
        for part in range(parts):
            for level in range(LEVELS):
                row = (part * LEVELS + level) * slice_rows
                key_ref[row : row + slice_rows, :] = part_refs[part][leaf * LEVELS + level]
        key_ref[node_rows:, :] = own_ref[leaf * leaf_rows : (leaf + 1) * leaf_rows, :]
        keys = key_ref[...]
        keys_ref[leaf] = keys
        query = query_ref[leaf * lines : (leaf + 1) * lines, :]
        grad = grad_ref[leaf * lines : (leaf + 1) * lines, :]
        scores = dot(keys, query, NT) * score_scale
        row_of = lax.broadcasted_iota(jnp.int32, (leaf_rows, lines), 1) // heads
        own_key = lax.broadcasted_iota(jnp.int32, (leaf_rows, lines), 0)
        own_scores = jnp.where(own_key <= row_of, scores[node_rows:], -jnp.inf)
        scores = jnp.concatenate([scores[:node_rows], own_scores], axis=0)
        top = jnp.max(scores, axis=0, keepdims=True)
        expo = jnp.exp(scores - top)
        live = lax.broadcasted_iota(jnp.int32, (1, lines), 1) // heads < len_ref[leaf]
        scale = jnp.where(live, 1.0, 0.0) / jnp.sum(expo, axis=0, keepdims=True)
        probs = expo * scale
        probs_b = probs.astype(jnp.bfloat16)
        probs_ref[leaf] = probs_b
        dprobs = dot(keys[:, :LAT], grad, NT)
        delta = jnp.sum(probs_b.astype(jnp.float32) * dprobs, axis=0, keepdims=True)
        dscore_ref[...] = (score_scale * probs * (dprobs - delta)).astype(jnp.bfloat16)
        dscores = dscore_ref[...]
        head_part = dot(dscores, query[:, :LAT], NN) + dot(probs_ref[leaf], grad, NN)
        tail_part = dot(dscores, query[:, LAT:], NN)
        for part in range(parts):
            for level in range(LEVELS):
                row = (part * LEVELS + level) * slice_rows
                ref = term_refs[part]
                ref[leaf * LEVELS + level, :, :LAT] = head_part[row : row + slice_rows].astype(ref.dtype)
                ref[leaf * LEVELS + level, :, LAT:] = tail_part[row : row + slice_rows].astype(ref.dtype)
        first = leaf * leaf_rows
        own_grad_ref[first : first + leaf_rows, :LAT] = head_part[node_rows:].astype(jnp.bfloat16)
        own_grad_ref[first : first + leaf_rows, LAT:] = tail_part[node_rows:].astype(jnp.bfloat16)


def grads(lengths, own, query, grad, parts, leaves, heads):
    slots, slice_rows, width = parts[0].shape
    rows = own.shape[0]
    lines = rows * heads // leaves
    total_keys = LEVELS * len(parts) * slice_rows + rows // leaves
    outs = [
        jax.ShapeDtypeStruct((slots, slice_rows, width), jnp.float32 if i == 0 else jnp.bfloat16)
        for i in range(len(parts))
    ] + [
        jax.ShapeDtypeStruct((rows, width), jnp.bfloat16),
        jax.ShapeDtypeStruct((leaves, total_keys, lines), jnp.bfloat16),
        jax.ShapeDtypeStruct((leaves, total_keys, width), jnp.bfloat16),
    ]
    return pl.pallas_call(
        functools.partial(grads_kernel, len(parts), leaves, heads),
        out_shape=outs,
        in_specs=[pl.BlockSpec(memory_space=pltpu.SMEM)] + vmem(3 + len(parts)),
        out_specs=vmem(len(outs)),
        scratch_shapes=[
            pltpu.VMEM((total_keys, width), jnp.bfloat16),
            pltpu.VMEM((total_keys, lines), jnp.bfloat16),
        ],
        compiler_params=pltpu.CompilerParams(vmem_limit_bytes=40 << 20),
        cost_estimate=cost(2 * rows * heads * total_keys * 4 * width, 8 << 20),
        name="attend_grads",
    )(lengths, own, query, grad, *parts)


def outputs_kernel(leaves, probs_ref, keys_ref, out_ref):
    lines = probs_ref.shape[2]
    for leaf in range(leaves):
        out = dot(probs_ref[leaf], keys_ref[leaf, :, :LAT], TN)
        out_ref[leaf * lines : (leaf + 1) * lines, :] = out.astype(jnp.bfloat16)


def outputs(probs, keys):
    leaves, total_keys, lines = probs.shape
    return pl.pallas_call(
        functools.partial(outputs_kernel, leaves),
        out_shape=jax.ShapeDtypeStruct((leaves * lines, LAT), jnp.bfloat16),
        in_specs=vmem(2),
        out_specs=vmem(1)[0],
        compiler_params=pltpu.CompilerParams(vmem_limit_bytes=24 << 20),
        cost_estimate=cost(2 * leaves * total_keys * lines * LAT, 4 << 20),
        name="attend_outputs",
    )(probs, keys)


def spread_kernel(shares, where_ref, *refs):
    share_refs, rest = refs[:shares], refs[shares:]
    keep_ref, send_refs, table_ref = rest[0], rest[1:-1], rest[-1]
    inner = keep_ref.shape[0]
    table_ref[...] = jnp.zeros_like(table_ref)
    for slot in range(share_refs[0].shape[0]):
        total = share_refs[0][slot]
        for ref in share_refs[1:]:
            total = total + ref[slot].astype(jnp.float32)
        table_ref[where_ref[slot]] += total
    keep_ref[...] = table_ref[:inner]
    for i, ref in enumerate(send_refs):
        ref[...] = table_ref[(i + 1) * inner : (i + 2) * inner].astype(jnp.bfloat16)


def spread(where, shares, outer, inner):
    block = shares[0].shape[1:]
    outs = [jax.ShapeDtypeStruct((inner,) + block, jnp.float32)] + [
        jax.ShapeDtypeStruct((inner,) + block, jnp.bfloat16)
    ] * (outer - 1)
    return pl.pallas_call(
        functools.partial(spread_kernel, len(shares)),
        out_shape=outs,
        in_specs=[pl.BlockSpec(memory_space=pltpu.SMEM)] + vmem(len(shares)),
        out_specs=vmem(len(outs)),
        scratch_shapes=[pltpu.VMEM((outer * inner,) + block, jnp.float32)],
        compiler_params=pltpu.CompilerParams(vmem_limit_bytes=40 << 20),
        name="spread_terms",
    )(where, *shares)


def merge_kernel(count, *refs):
    keep_ref, got_refs, out_refs = refs[0], refs[1:count], refs[count:]
    for i, ref in enumerate(out_refs):
        total = keep_ref[i]
        for got in got_refs:
            total = total + got[i].astype(jnp.float32)
        ref[0] = total.astype(ref.dtype)


def merge(keep, got):
    inner = keep.shape[0]
    block = (1,) + keep.shape[1:]
    outs = [jax.ShapeDtypeStruct(block, jnp.float32)] + [
        jax.ShapeDtypeStruct(block, jnp.bfloat16)
    ] * (inner - 1)
    return pl.pallas_call(
        functools.partial(merge_kernel, 1 + len(got)),
        out_shape=outs,
        in_specs=vmem(1 + len(got)),
        out_specs=vmem(len(outs)),
        compiler_params=pltpu.CompilerParams(vmem_limit_bytes=40 << 20),
        name="merge_terms",
    )(keep, *got)


def body(leaf_size, head_size, queries, leaf_latent, node_latent, grad_out, leaf_nodes, leaf_lengths):
    rows, heads, width = queries.shape
    leaves = leaf_nodes.shape[0]
    side = 1
    while side * side < leaf_size:
        side *= 2
    axes = ("leaf", "head")

    def step(value, which, distance):
        pairs = []
        for leaf in range(leaf_size):
            for head in range(head_size):
                far = (which + head) % 2 == 0
                target = leaf ^ (distance * side if far else distance)
                pairs.append((leaf * head_size + head, target * head_size + head))
        return lax.ppermute(value, axes, pairs)

    def swap(value, distance):
        return lax.ppermute(value, "head", [(i, i ^ distance) for i in range(head_size)])

    relative = leaf_nodes.reshape(-1) ^ lax.axis_index("leaf")
    far, near = relative // side, relative % side
    even = lax.axis_index("head") % 2 == 0
    where = jnp.where(even, near * side + far, far * side + near)

    order = list(range(side - 1, 0, -1))
    got = {d: step(node_latent, 0, d) for d in order}
    inner = jnp.concatenate([node_latent] + [got[d] for d in range(1, side)], axis=0)
    query = queries.reshape(rows * heads, width)
    inner, query, own = lax.optimization_barrier((inner, query, leaf_latent))
    got = {d: step(inner, 1, d) for d in order}
    table = jnp.concatenate([inner] + [got[d] for d in range(1, side)], axis=0)
    mine = select(where, table)
    parts = [mine] + [swap(mine, d) for d in range(1, head_size)]
    grad = grad_out.reshape(rows * heads, LAT)
    results = grads(leaf_lengths, own, query, grad, parts, leaves, heads)
    terms, (own_grad, probs, keys) = results[:head_size], results[head_size:]

    shares = [terms[0]] + [swap(terms[d], d) for d in range(1, head_size)]
    keep, *sends = spread(where, shares, side, side)
    got = {d: step(sends[d - 1], 1, d) for d in order}
    got = [got[d] for d in range(1, side)]
    attention = outputs(probs, keys).reshape(rows, heads, LAT)
    keep, *sends = merge(keep, got)
    got = {d: step(sends[d - 1], 0, d) for d in order}
    total = keep
    for d in range(1, side):
        total = total + got[d].astype(jnp.float32)
    node_grad = total.astype(jnp.bfloat16)

    leaf_grad = own_grad
    distance = 1
    while distance < head_size:
        leaf_grad = leaf_grad + swap(leaf_grad, distance)
        distance *= 2
    return (attention, node_grad, leaf_grad)


def solution(mesh):
    return jax.shard_map(
        functools.partial(body, mesh.shape["leaf"], mesh.shape["head"]),
        mesh=mesh,
        in_specs=(
            P("leaf", "head", None),
            P("leaf", None),
            P("leaf", "head", None),
            P("leaf", "head", None),
            P("leaf", None),
            P("leaf"),
        ),
        out_specs=(P("leaf", "head", None), P("leaf", "head", None), P("leaf", None)),
        check_vma=False,
    )
```

```python
import functools

import jax
import jax.numpy as jnp
from jax import lax
from jax.experimental import pallas as pl
from jax.experimental.pallas import tpu as pltpu
from jax.sharding import PartitionSpec as P

LAT = 512
LEVELS = 3

score_scale = 192.0 ** (-0.5)

NT = (((1,), (1,)), ((), ()))
NN = (((1,), (0,)), ((), ()))
TN = (((0,), (0,)), ((), ()))


def dot(a, b, dims):
    return lax.dot_general(a, b, dims, preferred_element_type=jnp.float32)


def vmem(count):
    return [pl.BlockSpec(memory_space=pltpu.VMEM)] * count


def cost(flops, moved):
    return pl.CostEstimate(flops=flops, bytes_accessed=moved, transcendentals=0)


def select_kernel(where_ref, table_ref, out_ref):
    for slot in range(out_ref.shape[0]):
        out_ref[slot] = table_ref[where_ref[slot]]


def select(where, table):
    slots = where.shape[0]
    shape = (slots,) + table.shape[1:]
    return pl.pallas_call(
        select_kernel,
        out_shape=jax.ShapeDtypeStruct(shape, table.dtype),
        in_specs=[pl.BlockSpec(memory_space=pltpu.SMEM)] + vmem(1),
        out_specs=vmem(1)[0],
        compiler_params=pltpu.CompilerParams(vmem_limit_bytes=4 << 20),
        name="select_nodes",
    )(where, table)


def pieces(slice_rows, width):
    lanes = 128
    full, tail = width // lanes, width % lanes
    if slice_rows % 16 or 2 * tail != lanes:
        return [(slice(0, slice_rows), slice(0, width), slice(0, slice_rows), slice(0, width))]
    out = []
    for j in range(full):
        out.append((slice(j * slice_rows, (j + 1) * slice_rows), slice(0, lanes), slice(0, slice_rows), slice(j * lanes, (j + 1) * lanes)))
    half = slice_rows // 2
    last = slice(full * slice_rows, full * slice_rows + half)
    for k in range(2):
        out.append((last, slice(k * tail, (k + 1) * tail), slice(k * half, (k + 1) * half), slice(full * lanes, width)))
    return out


def packed_shape(slice_rows, width):
    parts = pieces(slice_rows, width)
    return (max(p[0].stop for p in parts), max(p[1].stop for p in parts))


def pack_kernel(*refs):
    out_ref = refs[-1]
    for i, ref in enumerate(refs[:-1]):
        for prow, plane, row, col in pieces(*ref.shape[1:]):
            out_ref[i, prow, plane] = ref[0, row, col]


def pack(blocks):
    slice_rows, width = blocks[0].shape[1:]
    shape = (len(blocks),) + packed_shape(slice_rows, width)
    return pl.pallas_call(
        pack_kernel,
        out_shape=jax.ShapeDtypeStruct(shape, blocks[0].dtype),
        in_specs=vmem(len(blocks)),
        out_specs=vmem(1)[0],
        compiler_params=pltpu.CompilerParams(vmem_limit_bytes=4 << 20),
        name="pack_nodes",
    )(*blocks)


def store_terms(ref, first_slot, slice_rows, width, base, head_part, tail_part):
    for level in range(LEVELS):
        offset = base + level * slice_rows
        for prow, plane, row, col in pieces(slice_rows, width):
            rows = slice(offset + row.start, offset + row.stop)
            if col.start >= LAT:
                value = tail_part[rows, col.start - LAT : col.stop - LAT]
            elif col.stop <= LAT:
                value = head_part[rows, col]
            else:
                value = jnp.concatenate([head_part[rows, :], tail_part[rows, :]], axis=1)
            ref[first_slot + level, prow, plane] = value.astype(ref.dtype)


def attend_kernel(parts, leaves, heads, slice_rows, len_ref, own_ref, query_ref, grad_ref, *refs):
    part_refs, refs = refs[:parts], refs[parts:]
    term_refs, refs = refs[: parts - 1], refs[parts - 1 :]
    dscores_ref, probs_ref, keys_ref = refs
    width = own_ref.shape[1]
    leaf_rows = own_ref.shape[0] // leaves
    lines = leaf_rows * heads
    level_rows = LEVELS * slice_rows
    node_rows = parts * level_rows
    sent_rows = node_rows - level_rows
    order = list(range(1, parts)) + [0]
    for leaf in range(leaves):
        for place, part in enumerate(order):
            for level in range(LEVELS):
                offset = place * level_rows + level * slice_rows
                for prow, plane, row, col in pieces(slice_rows, width):
                    rows = slice(offset + row.start, offset + row.stop)
                    keys_ref[leaf, rows, col] = part_refs[part][leaf * LEVELS + level, prow, plane]
        keys_ref[leaf, node_rows:, :] = own_ref[leaf * leaf_rows : (leaf + 1) * leaf_rows, :]
        query = query_ref[leaf * lines : (leaf + 1) * lines, :]
        grad = grad_ref[leaf * lines : (leaf + 1) * lines, :]
        scores = dot(keys_ref[leaf], query, NT) * score_scale
        row_of = lax.broadcasted_iota(jnp.int32, (leaf_rows, lines), 1) // heads
        own_key = lax.broadcasted_iota(jnp.int32, (leaf_rows, lines), 0)
        own_scores = jnp.where(own_key <= row_of, scores[node_rows:], -jnp.inf)
        scores = jnp.concatenate([scores[:node_rows], own_scores], axis=0)
        top = jnp.max(scores, axis=0, keepdims=True)
        expo = jnp.exp(scores - top)
        live = lax.broadcasted_iota(jnp.int32, (1, lines), 1) // heads < len_ref[leaf]
        scale = jnp.where(live, 1.0, 0.0) / jnp.sum(expo, axis=0, keepdims=True)
        probs = expo * scale
        probs_b = probs.astype(jnp.bfloat16)
        probs_ref[leaf] = probs_b
        dprobs = dot(keys_ref[leaf, :, :LAT], grad, NT)
        delta = jnp.sum(probs_b.astype(jnp.float32) * dprobs, axis=0, keepdims=True)
        dscores_ref[leaf] = (score_scale * probs * (dprobs - delta)).astype(jnp.bfloat16)
        if parts > 1:
            head_part, tail_part = key_grads(dscores_ref[leaf, :sent_rows, :], probs_ref[leaf, :sent_rows, :], query, grad)
            for place in range(parts - 1):
                store_terms(term_refs[place], leaf * LEVELS, slice_rows, width, place * level_rows, head_part, tail_part)


def key_grads(dscores, probs_b, query, grad):
    head_part = dot(dscores, query[:, :LAT], NN) + dot(probs_b, grad, NN)
    return head_part, dot(dscores, query[:, LAT:], NN)


def attend(lengths, own, query, grad, parts, leaves, heads, slice_rows):
    rows, width = own.shape
    lines = rows * heads // leaves
    total_keys = LEVELS * len(parts) * slice_rows + rows // leaves
    outs = [jax.ShapeDtypeStruct(parts[0].shape, jnp.bfloat16)] * (len(parts) - 1) + [
        jax.ShapeDtypeStruct((leaves, total_keys, lines), jnp.bfloat16),
        jax.ShapeDtypeStruct((leaves, total_keys, lines), jnp.bfloat16),
        jax.ShapeDtypeStruct((leaves, total_keys, width), jnp.bfloat16),
    ]
    return pl.pallas_call(
        functools.partial(attend_kernel, len(parts), leaves, heads, slice_rows),
        out_shape=outs,
        in_specs=[pl.BlockSpec(memory_space=pltpu.SMEM)] + vmem(3 + len(parts)),
        out_specs=vmem(len(outs)),
        compiler_params=pltpu.CompilerParams(vmem_limit_bytes=40 << 20),
        cost_estimate=cost(2 * rows * heads * total_keys * 3 * width, 8 << 20),
        name="attend",
    )(lengths, own, query, grad, *parts)


def own_kernel(leaves, slice_rows, level_rows, query_ref, grad_ref, dscores_ref, probs_ref, term_ref, own_grad_ref):
    lines = query_ref.shape[0] // leaves
    width = query_ref.shape[1]
    leaf_rows = own_grad_ref.shape[0] // leaves
    first = dscores_ref.shape[1] - leaf_rows - level_rows
    for leaf in range(leaves):
        query = query_ref[leaf * lines : (leaf + 1) * lines, :]
        grad = grad_ref[leaf * lines : (leaf + 1) * lines, :]
        head_part, tail_part = key_grads(dscores_ref[leaf, first:, :], probs_ref[leaf, first:, :], query, grad)
        store_terms(term_ref, leaf * LEVELS, slice_rows, width, 0, head_part, tail_part)
        rows = slice(leaf * leaf_rows, (leaf + 1) * leaf_rows)
        own_grad_ref[rows, :LAT] = head_part[level_rows:].astype(jnp.bfloat16)
        own_grad_ref[rows, LAT:] = tail_part[level_rows:].astype(jnp.bfloat16)


def own_terms(query, grad, dscores, probs, block, slice_rows, rows):
    leaves, total_keys, lines = dscores.shape
    width = query.shape[1]
    level_rows = LEVELS * slice_rows
    outs = [
        jax.ShapeDtypeStruct(block, jnp.float32),
        jax.ShapeDtypeStruct((rows, width), jnp.bfloat16),
    ]
    return pl.pallas_call(
        functools.partial(own_kernel, leaves, slice_rows, level_rows),
        out_shape=outs,
        in_specs=vmem(4),
        out_specs=vmem(2),
        compiler_params=pltpu.CompilerParams(vmem_limit_bytes=24 << 20),
        cost_estimate=cost(2 * leaves * lines * (level_rows + rows // leaves) * 2 * width, 4 << 20),
        name="own_terms",
    )(query, grad, dscores, probs)


def outputs_kernel(leaves, probs_ref, keys_ref, out_ref):
    lines = probs_ref.shape[2]
    for leaf in range(leaves):
        out = dot(probs_ref[leaf], keys_ref[leaf, :, :LAT], TN)
        out_ref[leaf * lines : (leaf + 1) * lines, :] = out.astype(jnp.bfloat16)


def outputs(probs, keys):
    leaves, total_keys, lines = probs.shape
    return pl.pallas_call(
        functools.partial(outputs_kernel, leaves),
        out_shape=jax.ShapeDtypeStruct((leaves * lines, LAT), jnp.bfloat16),
        in_specs=vmem(2),
        out_specs=vmem(1)[0],
        compiler_params=pltpu.CompilerParams(vmem_limit_bytes=24 << 20),
        cost_estimate=cost(2 * leaves * total_keys * lines * LAT, 4 << 20),
        name="attend_outputs",
    )(probs, keys)


def spread_kernel(shares, leaves, where_ref, *refs):
    share_refs, out_refs = refs[:shares], refs[shares:]
    inner = out_refs[0].shape[0]
    for ref in out_refs:
        ref[...] = jnp.zeros_like(ref)
    for level in range(LEVELS):
        slots = [leaf * LEVELS + level for leaf in range(leaves)]
        totals = []
        for slot in slots:
            total = share_refs[0][slot]
            for ref in share_refs[1:]:
                total = total + ref[slot].astype(jnp.float32)
            totals.append(total)
        for i, slot in enumerate(slots):
            total = totals[i]
            for j, other in enumerate(slots):
                if j != i:
                    shared = where_ref[other] == where_ref[slot]
                    total = total + jnp.where(shared, totals[j], 0.0)
            total = total.astype(jnp.bfloat16)
            place = where_ref[slot]
            for k, ref in enumerate(out_refs):

                @pl.when(place // inner == k)
                def _(ref=ref, total=total, place=place):
                    ref[place % inner] = total


def spread(where, shares, outer, inner):
    block = shares[0].shape[1:]
    outs = [jax.ShapeDtypeStruct((inner,) + block, jnp.bfloat16)] * outer
    return pl.pallas_call(
        functools.partial(spread_kernel, len(shares), shares[0].shape[0] // LEVELS),
        out_shape=outs,
        in_specs=[pl.BlockSpec(memory_space=pltpu.SMEM)] + vmem(len(shares)),
        out_specs=vmem(len(outs)),
        compiler_params=pltpu.CompilerParams(vmem_limit_bytes=16 << 20),
        name="spread_terms",
    )(where, *shares)


def merge_kernel(count, *refs):
    got_refs, out_refs = refs[:count], refs[count:]
    for i, ref in enumerate(out_refs):
        total = got_refs[0][i].astype(jnp.float32)
        for got in got_refs[1:]:
            total = total + got[i].astype(jnp.float32)
        ref[0] = total.astype(ref.dtype)


def merge(got):
    inner = got[0].shape[0]
    block = (1,) + got[0].shape[1:]
    outs = [jax.ShapeDtypeStruct(block, jnp.float32)] + [
        jax.ShapeDtypeStruct(block, jnp.bfloat16)
    ] * (inner - 1)
    return pl.pallas_call(
        functools.partial(merge_kernel, len(got)),
        out_shape=outs,
        in_specs=vmem(len(got)),
        out_specs=vmem(len(outs)),
        compiler_params=pltpu.CompilerParams(vmem_limit_bytes=16 << 20),
        name="merge_terms",
    )(*got)


def finish_kernel(keep_ref, *refs):
    out_ref = refs[-1]
    for prow, plane, row, col in pieces(*out_ref.shape[1:]):
        total = keep_ref[0, prow, plane]
        for ref in refs[:-1]:
            total = total + ref[0, prow, plane].astype(jnp.float32)
        out_ref[0, row, col] = total.astype(jnp.bfloat16)


def finish(keep, got, shape):
    return pl.pallas_call(
        finish_kernel,
        out_shape=jax.ShapeDtypeStruct(shape, jnp.bfloat16),
        in_specs=vmem(1 + len(got)),
        out_specs=vmem(1)[0],
        compiler_params=pltpu.CompilerParams(vmem_limit_bytes=4 << 20),
        name="finish_nodes",
    )(keep, *got)


def body(leaf_size, head_size, queries, leaf_latent, node_latent, grad_out, leaf_nodes, leaf_lengths):
    rows, heads, width = queries.shape
    leaves = leaf_nodes.shape[0]
    side = 1
    while side * side < leaf_size:
        side *= 2
    axes = ("leaf", "head")

    def step(value, which, distance):
        pairs = []
        for leaf in range(leaf_size):
            for head in range(head_size):
                far = (which + head) % 2 == 0
                target = leaf ^ (distance * side if far else distance)
                pairs.append((leaf * head_size + head, target * head_size + head))
        return lax.ppermute(value, axes, pairs)

    def swap(value, distance):
        return lax.ppermute(value, "head", [(i, i ^ distance) for i in range(head_size)])

    relative = leaf_nodes.reshape(-1) ^ lax.axis_index("leaf")
    far, near = relative // side, relative % side
    even = lax.axis_index("head") % 2 == 0
    where = jnp.where(even, near * side + far, far * side + near)

    order = list(range(side - 1, 0, -1))
    got = {d: step(node_latent, 0, d) for d in order}
    query = queries.reshape(rows * heads, width)
    got, query, own = lax.optimization_barrier(([got[d] for d in range(1, side)], query, leaf_latent))
    inner = pack([node_latent] + got)
    got = {d: step(inner, 1, d) for d in order}
    table = jnp.concatenate([inner] + [got[d] for d in range(1, side)], axis=0)
    mine = select(where, table)
    parts = [mine] + [swap(mine, d) for d in range(1, head_size)]
    grad = grad_out.reshape(rows * heads, LAT)
    slice_rows = node_latent.shape[1]

    *terms, dscores, probs, keys = attend(leaf_lengths, own, query, grad, parts, leaves, heads, slice_rows)
    shares = [swap(terms[d - 1], d) for d in range(1, head_size)]
    mine, own_grad = own_terms(query, grad, dscores, probs, mine.shape, slice_rows, rows)
    sends = spread(where, [mine] + shares, side, side)
    sends, probs, own_grad = lax.optimization_barrier((sends, probs, own_grad))
    got = {d: step(sends[d], 1, d) for d in order}
    attention = outputs(probs, keys).reshape(rows, heads, LAT)
    got, attention = lax.optimization_barrier(([sends[0]] + [got[d] for d in range(1, side)], attention))
    keep, *sends = merge(got)
    got = {d: step(sends[d - 1], 0, d) for d in order}
    node_grad = finish(keep, [got[d] for d in range(1, side)], node_latent.shape)

    leaf_grad = own_grad
    distance = 1
    while distance < head_size:
        leaf_grad = leaf_grad + swap(leaf_grad, distance)
        distance *= 2
    return (attention, node_grad, leaf_grad)


def solution(mesh):
    return jax.shard_map(
        functools.partial(body, mesh.shape["leaf"], mesh.shape["head"]),
        mesh=mesh,
        in_specs=(
            P("leaf", "head", None),
            P("leaf", None),
            P("leaf", "head", None),
            P("leaf", "head", None),
            P("leaf", None),
            P("leaf"),
        ),
        out_specs=(P("leaf", "head", None), P("leaf", "head", None), P("leaf", None)),
        check_vma=False,
    )
```

```python
import functools

import jax
import jax.numpy as jnp
from jax import lax
from jax.experimental import pallas as pl
from jax.experimental.pallas import tpu as pltpu
from jax.sharding import PartitionSpec as P

LAT = 512
LEVELS = 3

score_scale = 192.0 ** (-0.5)

NT = (((1,), (1,)), ((), ()))
NN = (((1,), (0,)), ((), ()))
TN = (((0,), (0,)), ((), ()))


def dot(a, b, dims):
    return lax.dot_general(a, b, dims, preferred_element_type=jnp.float32)


def vmem(count):
    return [pl.BlockSpec(memory_space=pltpu.VMEM)] * count


def cost(flops, moved):
    return pl.CostEstimate(flops=flops, bytes_accessed=moved, transcendentals=0)


def select_kernel(where_ref, table_ref, out_ref):
    for slot in range(out_ref.shape[0]):
        out_ref[slot] = table_ref[where_ref[0, slot]]


def select(where, table):
    slots = where.shape[1]
    shape = (slots,) + table.shape[1:]
    return pl.pallas_call(
        select_kernel,
        out_shape=jax.ShapeDtypeStruct(shape, table.dtype),
        in_specs=vmem(2),
        out_specs=vmem(1)[0],
        compiler_params=pltpu.CompilerParams(vmem_limit_bytes=4 << 20),
        name="select_nodes",
    )(where, table)


def pieces(slice_rows, width):
    lanes = 128
    full, tail = width // lanes, width % lanes
    if slice_rows % 16 or 2 * tail != lanes:
        return [(slice(0, slice_rows), slice(0, width), slice(0, slice_rows), slice(0, width))]
    out = []
    for j in range(full):
        out.append((slice(j * slice_rows, (j + 1) * slice_rows), slice(0, lanes), slice(0, slice_rows), slice(j * lanes, (j + 1) * lanes)))
    half = slice_rows // 2
    last = slice(full * slice_rows, full * slice_rows + half)
    for k in range(2):
        out.append((last, slice(k * tail, (k + 1) * tail), slice(k * half, (k + 1) * half), slice(full * lanes, width)))
    return out


def packed_shape(slice_rows, width):
    parts = pieces(slice_rows, width)
    return (max(p[0].stop for p in parts), max(p[1].stop for p in parts))


def pack_kernel(*refs):
    out_ref = refs[-1]
    for i, ref in enumerate(refs[:-1]):
        for prow, plane, row, col in pieces(*ref.shape[1:]):
            out_ref[i, prow, plane] = ref[0, row, col]


def pack(blocks):
    slice_rows, width = blocks[0].shape[1:]
    shape = (len(blocks),) + packed_shape(slice_rows, width)
    return pl.pallas_call(
        pack_kernel,
        out_shape=jax.ShapeDtypeStruct(shape, blocks[0].dtype),
        in_specs=vmem(len(blocks)),
        out_specs=vmem(1)[0],
        compiler_params=pltpu.CompilerParams(vmem_limit_bytes=4 << 20),
        name="pack_nodes",
    )(*blocks)


def store_terms(ref, first_slot, slice_rows, width, base, head_part, tail_part):
    for level in range(LEVELS):
        offset = base + level * slice_rows
        for prow, plane, row, col in pieces(slice_rows, width):
            rows = slice(offset + row.start, offset + row.stop)
            if col.start >= LAT:
                value = tail_part[rows, col.start - LAT : col.stop - LAT]
            elif col.stop <= LAT:
                value = head_part[rows, col]
            else:
                value = jnp.concatenate([head_part[rows, :], tail_part[rows, :]], axis=1)
            ref[first_slot + level, prow, plane] = value.astype(ref.dtype)


def attend_kernel(parts, leaves, heads, slice_rows, live_ref, own_ref, query_ref, grad_ref, *refs):
    part_refs, refs = refs[:parts], refs[parts:]
    term_refs, refs = refs[: parts - 1], refs[parts - 1 :]
    dscores_ref, probs_ref, keys_ref = refs
    width = own_ref.shape[1]
    leaf_rows = own_ref.shape[0] // leaves
    lines = leaf_rows * heads
    level_rows = LEVELS * slice_rows
    node_rows = parts * level_rows
    sent_rows = node_rows - level_rows
    order = list(range(1, parts)) + [0]
    for leaf in range(leaves):
        for place, part in enumerate(order):
            for level in range(LEVELS):
                offset = place * level_rows + level * slice_rows
                for prow, plane, row, col in pieces(slice_rows, width):
                    rows = slice(offset + row.start, offset + row.stop)
                    keys_ref[leaf, rows, col] = part_refs[part][leaf * LEVELS + level, prow, plane]
        keys_ref[leaf, node_rows:, :] = own_ref[leaf * leaf_rows : (leaf + 1) * leaf_rows, :]
        query = query_ref[leaf * lines : (leaf + 1) * lines, :]
        grad = grad_ref[leaf * lines : (leaf + 1) * lines, :]
        scores = dot(keys_ref[leaf], query, NT) * score_scale
        row_of = lax.broadcasted_iota(jnp.int32, (leaf_rows, lines), 1) // heads
        own_key = lax.broadcasted_iota(jnp.int32, (leaf_rows, lines), 0)
        own_scores = jnp.where(own_key <= row_of, scores[node_rows:], -jnp.inf)
        scores = jnp.concatenate([scores[:node_rows], own_scores], axis=0)
        top = jnp.max(scores, axis=0, keepdims=True)
        expo = jnp.exp(scores - top)
        scale = live_ref[leaf] / jnp.sum(expo, axis=0, keepdims=True)
        probs = expo * scale
        probs_b = probs.astype(jnp.bfloat16)
        probs_ref[leaf] = probs_b
        dprobs = dot(keys_ref[leaf, :, :LAT], grad, NT)
        delta = jnp.sum(probs_b.astype(jnp.float32) * dprobs, axis=0, keepdims=True)
        dscores_ref[leaf] = (score_scale * probs * (dprobs - delta)).astype(jnp.bfloat16)
        if parts > 1:
            head_part, tail_part = key_grads(dscores_ref[leaf, :sent_rows, :], probs_ref[leaf, :sent_rows, :], query, grad)
            for place in range(parts - 1):
                store_terms(term_refs[place], leaf * LEVELS, slice_rows, width, place * level_rows, head_part, tail_part)


def key_grads(dscores, probs_b, query, grad):
    head_part = dot(dscores, query[:, :LAT], NN) + dot(probs_b, grad, NN)
    return head_part, dot(dscores, query[:, LAT:], NN)


def attend(live, own, query, grad, parts, leaves, heads, slice_rows):
    rows, width = own.shape
    lines = rows * heads // leaves
    total_keys = LEVELS * len(parts) * slice_rows + rows // leaves
    outs = [jax.ShapeDtypeStruct(parts[0].shape, jnp.bfloat16)] * (len(parts) - 1) + [
        jax.ShapeDtypeStruct((leaves, total_keys, lines), jnp.bfloat16),
        jax.ShapeDtypeStruct((leaves, total_keys, lines), jnp.bfloat16),
        jax.ShapeDtypeStruct((leaves, total_keys, width), jnp.bfloat16),
    ]
    return pl.pallas_call(
        functools.partial(attend_kernel, len(parts), leaves, heads, slice_rows),
        out_shape=outs,
        in_specs=vmem(4 + len(parts)),
        out_specs=vmem(len(outs)),
        compiler_params=pltpu.CompilerParams(vmem_limit_bytes=40 << 20),
        cost_estimate=cost(2 * rows * heads * total_keys * 3 * width, 8 << 20),
        name="attend",
    )(live, own, query, grad, *parts)


def own_kernel(leaves, slice_rows, level_rows, query_ref, grad_ref, dscores_ref, probs_ref, term_ref, own_grad_ref):
    lines = query_ref.shape[0] // leaves
    width = query_ref.shape[1]
    leaf_rows = own_grad_ref.shape[0] // leaves
    first = dscores_ref.shape[1] - leaf_rows - level_rows
    for leaf in range(leaves):
        query = query_ref[leaf * lines : (leaf + 1) * lines, :]
        grad = grad_ref[leaf * lines : (leaf + 1) * lines, :]
        head_part, tail_part = key_grads(dscores_ref[leaf, first:, :], probs_ref[leaf, first:, :], query, grad)
        store_terms(term_ref, leaf * LEVELS, slice_rows, width, 0, head_part, tail_part)
        rows = slice(leaf * leaf_rows, (leaf + 1) * leaf_rows)
        own_grad_ref[rows, :LAT] = head_part[level_rows:].astype(jnp.bfloat16)
        own_grad_ref[rows, LAT:] = tail_part[level_rows:].astype(jnp.bfloat16)


def own_terms(query, grad, dscores, probs, block, slice_rows, rows):
    leaves, total_keys, lines = dscores.shape
    width = query.shape[1]
    level_rows = LEVELS * slice_rows
    outs = [
        jax.ShapeDtypeStruct(block, jnp.float32),
        jax.ShapeDtypeStruct((rows, width), jnp.bfloat16),
    ]
    return pl.pallas_call(
        functools.partial(own_kernel, leaves, slice_rows, level_rows),
        out_shape=outs,
        in_specs=vmem(4),
        out_specs=vmem(2),
        compiler_params=pltpu.CompilerParams(vmem_limit_bytes=24 << 20),
        cost_estimate=cost(2 * leaves * lines * (level_rows + rows // leaves) * 2 * width, 4 << 20),
        name="own_terms",
    )(query, grad, dscores, probs)


def outputs_kernel(leaves, probs_ref, keys_ref, out_ref):
    lines = probs_ref.shape[2]
    for leaf in range(leaves):
        out = dot(probs_ref[leaf], keys_ref[leaf, :, :LAT], TN)
        out_ref[leaf * lines : (leaf + 1) * lines, :] = out.astype(jnp.bfloat16)


def outputs(probs, keys):
    leaves, total_keys, lines = probs.shape
    return pl.pallas_call(
        functools.partial(outputs_kernel, leaves),
        out_shape=jax.ShapeDtypeStruct((leaves * lines, LAT), jnp.bfloat16),
        in_specs=vmem(2),
        out_specs=vmem(1)[0],
        compiler_params=pltpu.CompilerParams(vmem_limit_bytes=24 << 20),
        cost_estimate=cost(2 * leaves * total_keys * lines * LAT, 4 << 20),
        name="attend_outputs",
    )(probs, keys)


def spread_kernel(shares, leaves, where_ref, *refs):
    share_refs, out_refs = refs[:shares], refs[shares:]
    inner = out_refs[0].shape[0]
    for ref in out_refs:
        ref[...] = jnp.zeros_like(ref)
    for level in range(LEVELS):
        slots = [leaf * LEVELS + level for leaf in range(leaves)]
        places = {slot: where_ref[0, slot] for slot in slots}
        totals = []
        for slot in slots:
            total = share_refs[0][slot]
            for ref in share_refs[1:]:
                total = total + ref[slot].astype(jnp.float32)
            totals.append(total)
        for i, slot in enumerate(slots):
            total = totals[i]
            for j, other in enumerate(slots):
                if j != i:
                    shared = places[other] == places[slot]
                    total = total + jnp.where(shared, totals[j], 0.0)
            total = total.astype(jnp.bfloat16)
            place = places[slot]
            for k, ref in enumerate(out_refs):

                @pl.when(place // inner == k)
                def _(ref=ref, total=total, place=place):
                    ref[place % inner] = total


def spread(where, shares, outer, inner):
    block = shares[0].shape[1:]
    outs = [jax.ShapeDtypeStruct((inner,) + block, jnp.bfloat16)] * outer
    return pl.pallas_call(
        functools.partial(spread_kernel, len(shares), shares[0].shape[0] // LEVELS),
        out_shape=outs,
        in_specs=vmem(1 + len(shares)),
        out_specs=vmem(len(outs)),
        compiler_params=pltpu.CompilerParams(vmem_limit_bytes=16 << 20),
        name="spread_terms",
    )(where, *shares)


def merge_kernel(count, *refs):
    got_refs, out_refs = refs[:count], refs[count:]
    for i, ref in enumerate(out_refs):
        total = got_refs[0][i].astype(jnp.float32)
        for got in got_refs[1:]:
            total = total + got[i].astype(jnp.float32)
        ref[0] = total.astype(ref.dtype)


def merge(got):
    inner = got[0].shape[0]
    block = (1,) + got[0].shape[1:]
    outs = [jax.ShapeDtypeStruct(block, jnp.float32)] + [
        jax.ShapeDtypeStruct(block, jnp.bfloat16)
    ] * (inner - 1)
    return pl.pallas_call(
        functools.partial(merge_kernel, len(got)),
        out_shape=outs,
        in_specs=vmem(len(got)),
        out_specs=vmem(len(outs)),
        compiler_params=pltpu.CompilerParams(vmem_limit_bytes=16 << 20),
        name="merge_terms",
    )(*got)


def finish_kernel(keep_ref, *refs):
    out_ref = refs[-1]
    for prow, plane, row, col in pieces(*out_ref.shape[1:]):
        total = keep_ref[0, prow, plane]
        for ref in refs[:-1]:
            total = total + ref[0, prow, plane].astype(jnp.float32)
        out_ref[0, row, col] = total.astype(jnp.bfloat16)


def finish(keep, got, shape):
    return pl.pallas_call(
        finish_kernel,
        out_shape=jax.ShapeDtypeStruct(shape, jnp.bfloat16),
        in_specs=vmem(1 + len(got)),
        out_specs=vmem(1)[0],
        compiler_params=pltpu.CompilerParams(vmem_limit_bytes=4 << 20),
        name="finish_nodes",
    )(keep, *got)


def body(leaf_size, head_size, queries, leaf_latent, node_latent, grad_out, leaf_nodes, leaf_lengths):
    rows, heads, width = queries.shape
    leaves = leaf_nodes.shape[0]
    side = 1
    while side * side < leaf_size:
        side *= 2
    axes = ("leaf", "head")

    def step(value, which, distance):
        pairs = []
        for leaf in range(leaf_size):
            for head in range(head_size):
                far = (which + head) % 2 == 0
                target = leaf ^ (distance * side if far else distance)
                pairs.append((leaf * head_size + head, target * head_size + head))
        return lax.ppermute(value, axes, pairs)

    def swap(value, distance):
        return lax.ppermute(value, "head", [(i, i ^ distance) for i in range(head_size)])

    relative = leaf_nodes.reshape(1, -1) ^ lax.axis_index("leaf")
    far, near = relative // side, relative % side
    even = lax.axis_index("head") % 2 == 0
    where = jnp.where(even, near * side + far, far * side + near)

    live = jnp.arange(rows * heads // leaves, dtype=jnp.int32) // heads < leaf_lengths[:, None, None]
    live = live.astype(jnp.float32)
    order = list(range(side - 1, 0, -1))
    got = {d: step(node_latent, 0, d) for d in order}
    query = queries.reshape(rows * heads, width)
    got, query, own = lax.optimization_barrier(([got[d] for d in range(1, side)], query, leaf_latent))
    inner = pack([node_latent] + got)
    got = {d: step(inner, 1, d) for d in order}
    table = jnp.concatenate([inner] + [got[d] for d in range(1, side)], axis=0)
    mine = select(where, table)
    parts = [mine] + [swap(mine, d) for d in range(1, head_size)]
    grad = grad_out.reshape(rows * heads, LAT)
    slice_rows = node_latent.shape[1]

    *terms, dscores, probs, keys = attend(live, own, query, grad, parts, leaves, heads, slice_rows)
    shares = [swap(terms[d - 1], d) for d in range(1, head_size)]
    mine, own_grad = own_terms(query, grad, dscores, probs, mine.shape, slice_rows, rows)
    sends = spread(where, [mine] + shares, side, side)
    sends, probs, own_grad = lax.optimization_barrier((sends, probs, own_grad))
    got = {d: step(sends[d], 1, d) for d in order}
    attention = outputs(probs, keys).reshape(rows, heads, LAT)
    got, attention = lax.optimization_barrier(([sends[0]] + [got[d] for d in order], attention))
    keep, *sends = merge(got)
    got = {d: step(sends[d - 1], 0, d) for d in order}
    node_grad = finish(keep, [got[d] for d in (*range(2, side), 1)], node_latent.shape)

    leaf_grad = own_grad
    distance = 1
    while distance < head_size:
        leaf_grad = leaf_grad + swap(leaf_grad, distance)
        distance *= 2
    return (attention, node_grad, leaf_grad)


def solution(mesh):
    return jax.shard_map(
        functools.partial(body, mesh.shape["leaf"], mesh.shape["head"]),
        mesh=mesh,
        in_specs=(
            P("leaf", "head", None),
            P("leaf", None),
            P("leaf", "head", None),
            P("leaf", "head", None),
            P("leaf", None),
            P("leaf"),
        ),
        out_specs=(P("leaf", "head", None), P("leaf", "head", None), P("leaf", None)),
        check_vma=False,
    )
```

```python
import functools

import jax
import jax.numpy as jnp
from jax import lax
from jax.experimental import pallas as pl
from jax.experimental.pallas import tpu as pltpu
from jax.sharding import PartitionSpec as P

LAT = 512
LEVELS = 3

score_scale = 192.0 ** (-0.5)

NT = (((1,), (1,)), ((), ()))
NN = (((1,), (0,)), ((), ()))
TN = (((0,), (0,)), ((), ()))


def dot(a, b, dims):
    return lax.dot_general(a, b, dims, preferred_element_type=jnp.float32)


def vmem(count):
    return [pl.BlockSpec(memory_space=pltpu.VMEM)] * count


def cost(flops, moved):
    return pl.CostEstimate(flops=flops, bytes_accessed=moved, transcendentals=0)


def select_kernel(where_ref, table_ref, out_ref):
    for slot in range(out_ref.shape[0]):
        out_ref[slot] = table_ref[where_ref[0, slot]]


def select(where, table):
    slots = where.shape[1]
    shape = (slots,) + table.shape[1:]
    return pl.pallas_call(
        select_kernel,
        out_shape=jax.ShapeDtypeStruct(shape, table.dtype),
        in_specs=vmem(2),
        out_specs=vmem(1)[0],
        compiler_params=pltpu.CompilerParams(vmem_limit_bytes=4 << 20),
        name="select_nodes",
    )(where, table)


def pieces(slice_rows, width):
    lanes = 128
    full, tail = width // lanes, width % lanes
    if slice_rows % 16 or 2 * tail != lanes:
        return [(slice(0, slice_rows), slice(0, width), slice(0, slice_rows), slice(0, width))]
    out = []
    for j in range(full):
        out.append((slice(j * slice_rows, (j + 1) * slice_rows), slice(0, lanes), slice(0, slice_rows), slice(j * lanes, (j + 1) * lanes)))
    half = slice_rows // 2
    last = slice(full * slice_rows, full * slice_rows + half)
    for k in range(2):
        out.append((last, slice(k * tail, (k + 1) * tail), slice(k * half, (k + 1) * half), slice(full * lanes, width)))
    return out


def packed_shape(slice_rows, width):
    parts = pieces(slice_rows, width)
    return (max(p[0].stop for p in parts), max(p[1].stop for p in parts))


def pack_kernel(*refs):
    out_ref = refs[-1]
    for i, ref in enumerate(refs[:-1]):
        for prow, plane, row, col in pieces(*ref.shape[1:]):
            out_ref[i, prow, plane] = ref[0, row, col]


def pack(blocks):
    slice_rows, width = blocks[0].shape[1:]
    shape = (len(blocks),) + packed_shape(slice_rows, width)
    return pl.pallas_call(
        pack_kernel,
        out_shape=jax.ShapeDtypeStruct(shape, blocks[0].dtype),
        in_specs=vmem(len(blocks)),
        out_specs=vmem(1)[0],
        compiler_params=pltpu.CompilerParams(vmem_limit_bytes=4 << 20),
        name="pack_nodes",
    )(*blocks)


def store_terms(ref, first_slot, slice_rows, width, base, head_part, tail_part):
    for level in range(LEVELS):
        offset = base + level * slice_rows
        for prow, plane, row, col in pieces(slice_rows, width):
            rows = slice(offset + row.start, offset + row.stop)
            if col.start >= LAT:
                value = tail_part[rows, col.start - LAT : col.stop - LAT]
            elif col.stop <= LAT:
                value = head_part[rows, col]
            else:
                value = jnp.concatenate([head_part[rows, :], tail_part[rows, :]], axis=1)
            ref[first_slot + level, prow, plane] = value.astype(ref.dtype)


def load_keys(ref, leaf, place, part_ref, slice_rows, width):
    for level in range(LEVELS):
        offset = (place * LEVELS + level) * slice_rows
        for prow, plane, row, col in pieces(slice_rows, width):
            rows = slice(offset + row.start, offset + row.stop)
            ref[leaf, rows, col] = part_ref[leaf * LEVELS + level, prow, plane]


def near_kernel(leaves, heads, slice_rows, part_ref, own_ref, query_ref, grad_ref, expo_ref, dprob_ref, top_ref, sum_ref, dot_ref, keys_ref):
    width = own_ref.shape[1]
    leaf_rows = own_ref.shape[0] // leaves
    lines = leaf_rows * heads
    level_rows = LEVELS * slice_rows
    for leaf in range(leaves):
        load_keys(keys_ref, leaf, 0, part_ref, slice_rows, width)
        keys_ref[leaf, level_rows:, :] = own_ref[leaf * leaf_rows : (leaf + 1) * leaf_rows, :]
        query = query_ref[leaf * lines : (leaf + 1) * lines, :]
        grad = grad_ref[leaf * lines : (leaf + 1) * lines, :]
        scores = dot(keys_ref[leaf], query, NT) * score_scale
        row_of = lax.broadcasted_iota(jnp.int32, (leaf_rows, lines), 1) // heads
        own_key = lax.broadcasted_iota(jnp.int32, (leaf_rows, lines), 0)
        own_scores = jnp.where(own_key <= row_of, scores[level_rows:], -jnp.inf)
        scores = jnp.concatenate([scores[:level_rows], own_scores], axis=0)
        top = jnp.max(scores, axis=0, keepdims=True)
        expo = jnp.exp(scores - top)
        dprobs = dot(keys_ref[leaf, :, :LAT], grad, NT)
        expo_ref[leaf] = expo
        dprob_ref[leaf] = dprobs
        top_ref[leaf] = top
        sum_ref[leaf] = jnp.sum(expo, axis=0, keepdims=True)
        dot_ref[leaf] = jnp.sum(expo * dprobs, axis=0, keepdims=True)


def near_scores(part, own, query, grad, leaves, heads, slice_rows):
    rows, width = own.shape
    lines = rows * heads // leaves
    near_rows = LEVELS * slice_rows + rows // leaves
    line = jax.ShapeDtypeStruct((leaves, 1, lines), jnp.float32)
    outs = [
        jax.ShapeDtypeStruct((leaves, near_rows, lines), jnp.float32),
        jax.ShapeDtypeStruct((leaves, near_rows, lines), jnp.float32),
        line,
        line,
        line,
        jax.ShapeDtypeStruct((leaves, near_rows, width), jnp.bfloat16),
    ]
    return pl.pallas_call(
        functools.partial(near_kernel, leaves, heads, slice_rows),
        out_shape=outs,
        in_specs=vmem(4),
        out_specs=vmem(len(outs)),
        compiler_params=pltpu.CompilerParams(vmem_limit_bytes=24 << 20),
        cost_estimate=cost(2 * rows * heads * near_rows * 2 * width, 4 << 20),
        name="near_scores",
    )(part, own, query, grad)


def attend_kernel(parts, leaves, slice_rows, live_ref, query_ref, grad_ref, top_ref, sum_ref, dot_ref, *refs):
    part_refs, refs = refs[:parts], refs[parts:]
    term_refs, refs = refs[:parts], refs[parts:]
    near_scale_ref, delta_ref, probs_ref, keys_ref, dscores_ref = refs
    width = query_ref.shape[1]
    lines = query_ref.shape[0] // leaves
    level_rows = LEVELS * slice_rows
    for leaf in range(leaves):
        query = query_ref[leaf * lines : (leaf + 1) * lines, :]
        grad = grad_ref[leaf * lines : (leaf + 1) * lines, :]
        for place in range(parts):
            load_keys(keys_ref, leaf, place, part_refs[place], slice_rows, width)
        scores = dot(keys_ref[leaf], query, NT) * score_scale
        dprobs = dot(keys_ref[leaf, :, :LAT], grad, NT)
        top = jnp.maximum(top_ref[leaf], jnp.max(scores, axis=0, keepdims=True))
        shift = jnp.exp(top_ref[leaf] - top)
        expo = jnp.exp(scores - top)
        total = shift * sum_ref[leaf] + jnp.sum(expo, axis=0, keepdims=True)
        scale = live_ref[leaf] / total
        delta = (shift * dot_ref[leaf] + jnp.sum(expo * dprobs, axis=0, keepdims=True)) * scale
        near_scale_ref[leaf] = shift * scale
        delta_ref[leaf] = delta
        probs = expo * scale
        probs_ref[leaf] = probs.astype(jnp.bfloat16)
        dscores_ref[...] = (score_scale * probs * (dprobs - delta)).astype(jnp.bfloat16)
        head_part, tail_part = key_grads(dscores_ref[...], probs_ref[leaf], query, grad)
        for place in range(parts):
            store_terms(term_refs[place], leaf * LEVELS, slice_rows, width, place * level_rows, head_part, tail_part)


def key_grads(dscores, probs_b, query, grad):
    head_part = dot(dscores, query[:, :LAT], NN) + dot(probs_b, grad, NN)
    return head_part, dot(dscores, query[:, LAT:], NN)


def attend(live, query, grad, stats, parts, leaves, slice_rows):
    width = query.shape[1]
    lines = live.shape[2]
    sent_rows = LEVELS * len(parts) * slice_rows
    line = jax.ShapeDtypeStruct((leaves, 1, lines), jnp.float32)
    outs = [jax.ShapeDtypeStruct(part.shape, jnp.bfloat16) for part in parts] + [
        line,
        line,
        jax.ShapeDtypeStruct((leaves, sent_rows, lines), jnp.bfloat16),
        jax.ShapeDtypeStruct((leaves, sent_rows, width), jnp.bfloat16),
    ]
    return pl.pallas_call(
        functools.partial(attend_kernel, len(parts), leaves, slice_rows),
        out_shape=outs,
        in_specs=vmem(6 + len(parts)),
        out_specs=vmem(len(outs)),
        scratch_shapes=[pltpu.VMEM((sent_rows, lines), jnp.bfloat16)],
        compiler_params=pltpu.CompilerParams(vmem_limit_bytes=40 << 20),
        cost_estimate=cost(2 * leaves * lines * sent_rows * 4 * width, 8 << 20),
        name="attend",
    )(live, query, grad, *stats, *parts)


def own_kernel(leaves, slice_rows, query_ref, grad_ref, expo_ref, dprob_ref, scale_ref, delta_ref, term_ref, own_grad_ref, probs_ref, *refs):
    dscores_ref = refs[-1]
    for ref in refs[:-1]:
        ref[...] = jnp.zeros_like(ref)
    lines = query_ref.shape[0] // leaves
    width = query_ref.shape[1]
    leaf_rows = own_grad_ref.shape[0] // leaves
    level_rows = LEVELS * slice_rows
    for leaf in range(leaves):
        query = query_ref[leaf * lines : (leaf + 1) * lines, :]
        grad = grad_ref[leaf * lines : (leaf + 1) * lines, :]
        probs = expo_ref[leaf] * scale_ref[leaf]
        probs_ref[leaf] = probs.astype(jnp.bfloat16)
        dscores_ref[...] = (score_scale * probs * (dprob_ref[leaf] - delta_ref[leaf])).astype(jnp.bfloat16)
        head_part, tail_part = key_grads(dscores_ref[...], probs_ref[leaf], query, grad)
        store_terms(term_ref, leaf * LEVELS, slice_rows, width, 0, head_part, tail_part)
        rows = slice(leaf * leaf_rows, (leaf + 1) * leaf_rows)
        own_grad_ref[rows, :LAT] = head_part[level_rows:].astype(jnp.bfloat16)
        own_grad_ref[rows, LAT:] = tail_part[level_rows:].astype(jnp.bfloat16)


def own_terms(query, grad, expo, dprobs, scale, delta, block, slice_rows, rows, side):
    leaves, near_rows, lines = expo.shape
    width = query.shape[1]
    outs = [
        jax.ShapeDtypeStruct(block, jnp.float32),
        jax.ShapeDtypeStruct((rows, width), jnp.bfloat16),
        jax.ShapeDtypeStruct(expo.shape, jnp.bfloat16),
    ] + [jax.ShapeDtypeStruct((side,) + block[1:], jnp.bfloat16)] * side
    return pl.pallas_call(
        functools.partial(own_kernel, leaves, slice_rows),
        out_shape=outs,
        in_specs=vmem(6),
        out_specs=vmem(len(outs)),
        scratch_shapes=[pltpu.VMEM((near_rows, lines), jnp.bfloat16)],
        compiler_params=pltpu.CompilerParams(vmem_limit_bytes=24 << 20),
        cost_estimate=cost(2 * leaves * lines * near_rows * 2 * width, 4 << 20),
        name="own_terms",
    )(query, grad, expo, dprobs, scale, delta)


def outputs_kernel(leaves, probs_ref, keys_ref, near_probs_ref, near_keys_ref, out_ref):
    lines = probs_ref.shape[2]
    for leaf in range(leaves):
        out = dot(probs_ref[leaf], keys_ref[leaf, :, :LAT], TN)
        out = out + dot(near_probs_ref[leaf], near_keys_ref[leaf, :, :LAT], TN)
        out_ref[leaf * lines : (leaf + 1) * lines, :] = out.astype(jnp.bfloat16)


def outputs(probs, keys, near_probs, near_keys):
    leaves, sent_rows, lines = probs.shape
    total_keys = sent_rows + near_probs.shape[1]
    return pl.pallas_call(
        functools.partial(outputs_kernel, leaves),
        out_shape=jax.ShapeDtypeStruct((leaves * lines, LAT), jnp.bfloat16),
        in_specs=vmem(4),
        out_specs=vmem(1)[0],
        compiler_params=pltpu.CompilerParams(vmem_limit_bytes=24 << 20),
        cost_estimate=cost(2 * leaves * total_keys * lines * LAT, 4 << 20),
        name="attend_outputs",
    )(probs, keys, near_probs, near_keys)


def spread_kernel(shares, leaves, where_ref, *refs):
    share_refs, refs = refs[:shares], refs[shares:]
    out_refs = refs[len(refs) // 2 :]
    inner = out_refs[0].shape[0]
    for level in range(LEVELS):
        slots = [leaf * LEVELS + level for leaf in range(leaves)]
        places = {slot: where_ref[0, slot] for slot in slots}
        totals = []
        for slot in slots:
            total = share_refs[0][slot]
            for ref in share_refs[1:]:
                total = total + ref[slot].astype(jnp.float32)
            totals.append(total)
        for i, slot in enumerate(slots):
            total = totals[i]
            for j, other in enumerate(slots):
                if j != i:
                    shared = places[other] == places[slot]
                    total = total + jnp.where(shared, totals[j], 0.0)
            total = total.astype(jnp.bfloat16)
            place = places[slot]
            for k, ref in enumerate(out_refs):

                @pl.when(place // inner == k)
                def _(ref=ref, total=total, place=place):
                    ref[place % inner] = total


def spread(where, shares, zeros):
    first = 1 + len(shares)
    return pl.pallas_call(
        functools.partial(spread_kernel, len(shares), shares[0].shape[0] // LEVELS),
        out_shape=[jax.ShapeDtypeStruct(zero.shape, zero.dtype) for zero in zeros],
        in_specs=vmem(first + len(zeros)),
        out_specs=vmem(len(zeros)),
        input_output_aliases={first + i: i for i in range(len(zeros))},
        compiler_params=pltpu.CompilerParams(vmem_limit_bytes=16 << 20),
        name="spread_terms",
    )(where, *shares, *zeros)


def merge_kernel(count, *refs):
    got_refs, out_refs = refs[:count], refs[count:]
    for i, ref in enumerate(out_refs):
        total = got_refs[0][i].astype(jnp.float32)
        for got in got_refs[1:]:
            total = total + got[i].astype(jnp.float32)
        ref[0] = total.astype(ref.dtype)


def merge(got):
    inner = got[0].shape[0]
    block = (1,) + got[0].shape[1:]
    outs = [jax.ShapeDtypeStruct(block, jnp.float32)] + [
        jax.ShapeDtypeStruct(block, jnp.bfloat16)
    ] * (inner - 1)
    return pl.pallas_call(
        functools.partial(merge_kernel, len(got)),
        out_shape=outs,
        in_specs=vmem(len(got)),
        out_specs=vmem(len(outs)),
        compiler_params=pltpu.CompilerParams(vmem_limit_bytes=16 << 20),
        name="merge_terms",
    )(*got)


def finish_kernel(keep_ref, *refs):
    out_ref = refs[-1]
    for prow, plane, row, col in pieces(*out_ref.shape[1:]):
        total = keep_ref[0, prow, plane]
        for ref in refs[:-1]:
            total = total + ref[0, prow, plane].astype(jnp.float32)
        out_ref[0, row, col] = total.astype(jnp.bfloat16)


def finish(keep, got, shape):
    return pl.pallas_call(
        finish_kernel,
        out_shape=jax.ShapeDtypeStruct(shape, jnp.bfloat16),
        in_specs=vmem(1 + len(got)),
        out_specs=vmem(1)[0],
        compiler_params=pltpu.CompilerParams(vmem_limit_bytes=4 << 20),
        name="finish_nodes",
    )(keep, *got)


def body(leaf_size, head_size, queries, leaf_latent, node_latent, grad_out, leaf_nodes, leaf_lengths):
    rows, heads, width = queries.shape
    leaves = leaf_nodes.shape[0]
    side = 1
    while side * side < leaf_size:
        side *= 2
    axes = ("leaf", "head")

    def step(value, which, distance):
        pairs = []
        for leaf in range(leaf_size):
            for head in range(head_size):
                far = (which + head) % 2 == 0
                target = leaf ^ (distance * side if far else distance)
                pairs.append((leaf * head_size + head, target * head_size + head))
        return lax.ppermute(value, axes, pairs)

    def swap(value, distance):
        return lax.ppermute(value, "head", [(i, i ^ distance) for i in range(head_size)])

    relative = leaf_nodes.reshape(1, -1) ^ lax.axis_index("leaf")
    far, near = relative // side, relative % side
    even = lax.axis_index("head") % 2 == 0
    where = jnp.where(even, near * side + far, far * side + near)

    live = jnp.arange(rows * heads // leaves, dtype=jnp.int32) // heads < leaf_lengths[:, None, None]
    live = live.astype(jnp.float32)
    order = list(range(side - 1, 0, -1))
    got = {d: step(node_latent, 0, d) for d in order}
    query = queries.reshape(rows * heads, width)
    got, query, own = lax.optimization_barrier(([got[d] for d in range(1, side)], query, leaf_latent))
    inner = pack([node_latent] + got)
    got = {d: step(inner, 1, d) for d in order}
    table = jnp.concatenate([inner] + [got[d] for d in range(1, side)], axis=0)
    mine = select(where, table)
    parts = [swap(mine, d) for d in range(1, head_size)]
    grad = grad_out.reshape(rows * heads, LAT)
    slice_rows = node_latent.shape[1]

    expo, dprobs, *stats, near_keys = near_scores(mine, own, query, grad, leaves, heads, slice_rows)
    *terms, scale, delta, probs, keys = attend(live, query, grad, stats, parts, leaves, slice_rows)
    shares = [swap(terms[d - 1], d) for d in range(1, head_size)]
    mine, own_grad, near_probs, *zeros = own_terms(query, grad, expo, dprobs, scale, delta, mine.shape, slice_rows, rows, side)
    sends = spread(where, [mine] + shares, zeros)
    sends, probs, own_grad = lax.optimization_barrier((sends, probs, own_grad))
    got = {d: step(sends[d], 1, d) for d in order}
    attention = outputs(probs, keys, near_probs, near_keys).reshape(rows, heads, LAT)
    got, attention = lax.optimization_barrier(([sends[0]] + [got[d] for d in order], attention))
    keep, *sends = merge(got)
    got = {d: step(sends[d - 1], 0, d) for d in order}
    node_grad = finish(keep, [got[d] for d in (*range(2, side), 1)], node_latent.shape)

    leaf_grad = own_grad
    distance = 1
    while distance < head_size:
        leaf_grad = leaf_grad + swap(leaf_grad, distance)
        distance *= 2
    return (attention, node_grad, leaf_grad)


def solution(mesh):
    return jax.shard_map(
        functools.partial(body, mesh.shape["leaf"], mesh.shape["head"]),
        mesh=mesh,
        in_specs=(
            P("leaf", "head", None),
            P("leaf", None),
            P("leaf", "head", None),
            P("leaf", "head", None),
            P("leaf", None),
            P("leaf"),
        ),
        out_specs=(P("leaf", "head", None), P("leaf", "head", None), P("leaf", None)),
        check_vma=False,
    )
```

```python
import functools

import jax
import jax.numpy as jnp
from jax import lax
from jax.experimental import pallas as pl
from jax.experimental.pallas import tpu as pltpu
from jax.sharding import PartitionSpec as P

LAT = 512
LEVELS = 3

score_scale = 192.0 ** (-0.5)

NT = (((1,), (1,)), ((), ()))
NN = (((1,), (0,)), ((), ()))
TN = (((0,), (0,)), ((), ()))


def dot(a, b, dims):
    return lax.dot_general(a, b, dims, preferred_element_type=jnp.float32)


def vmem(count):
    return [pl.BlockSpec(memory_space=pltpu.VMEM)] * count


def cost(flops, moved):
    return pl.CostEstimate(flops=flops, bytes_accessed=moved, transcendentals=0)


def select_kernel(where_ref, table_ref, out_ref):
    for slot in range(out_ref.shape[0]):
        out_ref[slot] = table_ref[where_ref[0, slot]]


def select(where, table):
    slots = where.shape[1]
    shape = (slots,) + table.shape[1:]
    return pl.pallas_call(
        select_kernel,
        out_shape=jax.ShapeDtypeStruct(shape, table.dtype),
        in_specs=vmem(2),
        out_specs=vmem(1)[0],
        compiler_params=pltpu.CompilerParams(vmem_limit_bytes=4 << 20),
        name="select_nodes",
    )(where, table)


def pieces(slice_rows, width):
    lanes = 128
    full, tail = width // lanes, width % lanes
    if slice_rows % 16 or 2 * tail != lanes:
        return [(slice(0, slice_rows), slice(0, width), slice(0, slice_rows), slice(0, width))]
    out = []
    for j in range(full):
        out.append((slice(j * slice_rows, (j + 1) * slice_rows), slice(0, lanes), slice(0, slice_rows), slice(j * lanes, (j + 1) * lanes)))
    half = slice_rows // 2
    last = slice(full * slice_rows, full * slice_rows + half)
    for k in range(2):
        out.append((last, slice(k * tail, (k + 1) * tail), slice(k * half, (k + 1) * half), slice(full * lanes, width)))
    return out


def packed_shape(slice_rows, width):
    parts = pieces(slice_rows, width)
    return (max(p[0].stop for p in parts), max(p[1].stop for p in parts))


def pack_kernel(places, *refs):
    out_ref = refs[-1]
    for i, ref in zip(places, refs[:-1]):
        for prow, plane, row, col in pieces(*ref.shape[1:]):
            out_ref[i, prow, plane] = ref[0, row, col]


def pack(blocks, places):
    slice_rows, width = blocks[0].shape[1:]
    shape = (len(blocks),) + packed_shape(slice_rows, width)
    return pl.pallas_call(
        functools.partial(pack_kernel, places),
        out_shape=jax.ShapeDtypeStruct(shape, blocks[0].dtype),
        in_specs=vmem(len(blocks)),
        out_specs=vmem(1)[0],
        compiler_params=pltpu.CompilerParams(vmem_limit_bytes=4 << 20),
        name="pack_nodes",
    )(*blocks)


def store_terms(ref, first_slot, slice_rows, width, base, head_part, tail_part):
    for level in range(LEVELS):
        offset = base + level * slice_rows
        for prow, plane, row, col in pieces(slice_rows, width):
            rows = slice(offset + row.start, offset + row.stop)
            if col.start >= LAT:
                value = tail_part[rows, col.start - LAT : col.stop - LAT]
            elif col.stop <= LAT:
                value = head_part[rows, col]
            else:
                value = jnp.concatenate([head_part[rows, :], tail_part[rows, :]], axis=1)
            ref[first_slot + level, prow, plane] = value.astype(ref.dtype)


def load_keys(ref, leaf, place, part_ref, slice_rows, width):
    for level in range(LEVELS):
        offset = (place * LEVELS + level) * slice_rows
        for prow, plane, row, col in pieces(slice_rows, width):
            rows = slice(offset + row.start, offset + row.stop)
            ref[leaf, rows, col] = part_ref[leaf * LEVELS + level, prow, plane]


def near_kernel(leaves, heads, slice_rows, part_ref, own_ref, query_ref, grad_ref, expo_ref, dprob_ref, top_ref, sum_ref, dot_ref, keys_ref):
    width = own_ref.shape[1]
    leaf_rows = own_ref.shape[0] // leaves
    lines = leaf_rows * heads
    level_rows = LEVELS * slice_rows
    for leaf in range(leaves):
        load_keys(keys_ref, leaf, 0, part_ref, slice_rows, width)
        keys_ref[leaf, level_rows:, :] = own_ref[leaf * leaf_rows : (leaf + 1) * leaf_rows, :]
        query = query_ref[leaf * lines : (leaf + 1) * lines, :]
        grad = grad_ref[leaf * lines : (leaf + 1) * lines, :]
        scores = dot(keys_ref[leaf], query, NT) * score_scale
        row_of = lax.broadcasted_iota(jnp.int32, (leaf_rows, lines), 1) // heads
        own_key = lax.broadcasted_iota(jnp.int32, (leaf_rows, lines), 0)
        own_scores = jnp.where(own_key <= row_of, scores[level_rows:], -jnp.inf)
        scores = jnp.concatenate([scores[:level_rows], own_scores], axis=0)
        top = jnp.max(scores, axis=0, keepdims=True)
        expo = jnp.exp(scores - top)
        dprobs = dot(keys_ref[leaf, :, :LAT], grad, NT)
        expo_ref[leaf] = expo
        dprob_ref[leaf] = dprobs
        top_ref[leaf] = top
        sum_ref[leaf] = jnp.sum(expo, axis=0, keepdims=True)
        dot_ref[leaf] = jnp.sum(expo * dprobs, axis=0, keepdims=True)


def near_scores(part, own, query, grad, leaves, heads, slice_rows):
    rows, width = own.shape
    lines = rows * heads // leaves
    near_rows = LEVELS * slice_rows + rows // leaves
    line = jax.ShapeDtypeStruct((leaves, 1, lines), jnp.float32)
    outs = [
        jax.ShapeDtypeStruct((leaves, near_rows, lines), jnp.float32),
        jax.ShapeDtypeStruct((leaves, near_rows, lines), jnp.float32),
        line,
        line,
        line,
        jax.ShapeDtypeStruct((leaves, near_rows, width), jnp.bfloat16),
    ]
    return pl.pallas_call(
        functools.partial(near_kernel, leaves, heads, slice_rows),
        out_shape=outs,
        in_specs=vmem(4),
        out_specs=vmem(len(outs)),
        compiler_params=pltpu.CompilerParams(vmem_limit_bytes=24 << 20),
        cost_estimate=cost(2 * rows * heads * near_rows * 2 * width, 4 << 20),
        name="near_scores",
    )(part, own, query, grad)


def attend_kernel(parts, leaves, slice_rows, live_ref, query_ref, grad_ref, top_ref, sum_ref, dot_ref, *refs):
    part_refs, refs = refs[:parts], refs[parts:]
    term_refs, refs = refs[:parts], refs[parts:]
    near_scale_ref, delta_ref, probs_ref, keys_ref, dscores_ref = refs
    width = query_ref.shape[1]
    lines = query_ref.shape[0] // leaves
    level_rows = LEVELS * slice_rows
    for leaf in range(leaves):
        query = query_ref[leaf * lines : (leaf + 1) * lines, :]
        grad = grad_ref[leaf * lines : (leaf + 1) * lines, :]
        for place in range(parts):
            load_keys(keys_ref, leaf, place, part_refs[place], slice_rows, width)
        scores = dot(keys_ref[leaf], query, NT) * score_scale
        dprobs = dot(keys_ref[leaf, :, :LAT], grad, NT)
        top = jnp.maximum(top_ref[leaf], jnp.max(scores, axis=0, keepdims=True))
        shift = jnp.exp(top_ref[leaf] - top)
        expo = jnp.exp(scores - top)
        total = shift * sum_ref[leaf] + jnp.sum(expo, axis=0, keepdims=True)
        scale = live_ref[leaf] / total
        delta = (shift * dot_ref[leaf] + jnp.sum(expo * dprobs, axis=0, keepdims=True)) * scale
        near_scale_ref[leaf] = shift * scale
        delta_ref[leaf] = delta
        probs = expo * scale
        probs_ref[leaf] = probs.astype(jnp.bfloat16)
        dscores_ref[...] = (score_scale * probs * (dprobs - delta)).astype(jnp.bfloat16)
        head_part, tail_part = key_grads(dscores_ref[...], probs_ref[leaf], query, grad)
        for place in range(parts):
            store_terms(term_refs[place], leaf * LEVELS, slice_rows, width, place * level_rows, head_part, tail_part)


def key_grads(dscores, probs_b, query, grad):
    head_part = dot(dscores, query[:, :LAT], NN) + dot(probs_b, grad, NN)
    return head_part, dot(dscores, query[:, LAT:], NN)


def attend(live, query, grad, stats, parts, leaves, slice_rows):
    width = query.shape[1]
    lines = live.shape[2]
    sent_rows = LEVELS * len(parts) * slice_rows
    line = jax.ShapeDtypeStruct((leaves, 1, lines), jnp.float32)
    outs = [jax.ShapeDtypeStruct(part.shape, jnp.bfloat16) for part in parts] + [
        line,
        line,
        jax.ShapeDtypeStruct((leaves, sent_rows, lines), jnp.bfloat16),
        jax.ShapeDtypeStruct((leaves, sent_rows, width), jnp.bfloat16),
    ]
    return pl.pallas_call(
        functools.partial(attend_kernel, len(parts), leaves, slice_rows),
        out_shape=outs,
        in_specs=vmem(6 + len(parts)),
        out_specs=vmem(len(outs)),
        scratch_shapes=[pltpu.VMEM((sent_rows, lines), jnp.bfloat16)],
        compiler_params=pltpu.CompilerParams(vmem_limit_bytes=40 << 20),
        cost_estimate=cost(2 * leaves * lines * sent_rows * 4 * width, 8 << 20),
        name="attend",
    )(live, query, grad, *stats, *parts)


def own_kernel(leaves, slice_rows, query_ref, grad_ref, expo_ref, dprob_ref, scale_ref, delta_ref, term_ref, own_grad_ref, probs_ref, *refs):
    dscores_ref = refs[-1]
    for ref in refs[:-1]:
        ref[...] = jnp.zeros_like(ref)
    lines = query_ref.shape[0] // leaves
    width = query_ref.shape[1]
    leaf_rows = own_grad_ref.shape[0] // leaves
    level_rows = LEVELS * slice_rows
    for leaf in range(leaves):
        query = query_ref[leaf * lines : (leaf + 1) * lines, :]
        grad = grad_ref[leaf * lines : (leaf + 1) * lines, :]
        probs = expo_ref[leaf] * scale_ref[leaf]
        probs_ref[leaf] = probs.astype(jnp.bfloat16)
        dscores_ref[...] = (score_scale * probs * (dprob_ref[leaf] - delta_ref[leaf])).astype(jnp.bfloat16)
        head_part, tail_part = key_grads(dscores_ref[...], probs_ref[leaf], query, grad)
        store_terms(term_ref, leaf * LEVELS, slice_rows, width, 0, head_part, tail_part)
        rows = slice(leaf * leaf_rows, (leaf + 1) * leaf_rows)
        own_grad_ref[rows, :LAT] = head_part[level_rows:].astype(jnp.bfloat16)
        own_grad_ref[rows, LAT:] = tail_part[level_rows:].astype(jnp.bfloat16)


def own_terms(query, grad, expo, dprobs, scale, delta, block, slice_rows, rows, side):
    leaves, near_rows, lines = expo.shape
    width = query.shape[1]
    outs = [
        jax.ShapeDtypeStruct(block, jnp.float32),
        jax.ShapeDtypeStruct((rows, width), jnp.bfloat16),
        jax.ShapeDtypeStruct(expo.shape, jnp.bfloat16),
    ] + [jax.ShapeDtypeStruct((side,) + block[1:], jnp.bfloat16)] * side
    return pl.pallas_call(
        functools.partial(own_kernel, leaves, slice_rows),
        out_shape=outs,
        in_specs=vmem(6),
        out_specs=vmem(len(outs)),
        scratch_shapes=[pltpu.VMEM((near_rows, lines), jnp.bfloat16)],
        compiler_params=pltpu.CompilerParams(vmem_limit_bytes=24 << 20),
        cost_estimate=cost(2 * leaves * lines * near_rows * 2 * width, 4 << 20),
        name="own_terms",
    )(query, grad, expo, dprobs, scale, delta)


def outputs_kernel(leaves, probs_ref, keys_ref, near_probs_ref, near_keys_ref, out_ref):
    lines = probs_ref.shape[2]
    for leaf in range(leaves):
        out = dot(probs_ref[leaf], keys_ref[leaf, :, :LAT], TN)
        out = out + dot(near_probs_ref[leaf], near_keys_ref[leaf, :, :LAT], TN)
        out_ref[leaf * lines : (leaf + 1) * lines, :] = out.astype(jnp.bfloat16)


def outputs(probs, keys, near_probs, near_keys):
    leaves, sent_rows, lines = probs.shape
    total_keys = sent_rows + near_probs.shape[1]
    return pl.pallas_call(
        functools.partial(outputs_kernel, leaves),
        out_shape=jax.ShapeDtypeStruct((leaves * lines, LAT), jnp.bfloat16),
        in_specs=vmem(4),
        out_specs=vmem(1)[0],
        compiler_params=pltpu.CompilerParams(vmem_limit_bytes=24 << 20),
        cost_estimate=cost(2 * leaves * total_keys * lines * LAT, 4 << 20),
        name="attend_outputs",
    )(probs, keys, near_probs, near_keys)


def spread_kernel(shares, leaves, where_ref, *refs):
    share_refs, refs = refs[:shares], refs[shares:]
    out_refs = refs[len(refs) // 2 :]
    inner = out_refs[0].shape[0]
    for level in range(LEVELS):
        slots = [leaf * LEVELS + level for leaf in range(leaves)]
        places = {slot: where_ref[0, slot] for slot in slots}
        totals = []
        for slot in slots:
            total = share_refs[0][slot]
            for ref in share_refs[1:]:
                total = total + ref[slot].astype(jnp.float32)
            totals.append(total)
        for i, slot in enumerate(slots):
            total = totals[i]
            for j, other in enumerate(slots):
                if j != i:
                    shared = places[other] == places[slot]
                    total = total + jnp.where(shared, totals[j], 0.0)
            total = total.astype(jnp.bfloat16)
            place = places[slot]
            for k, ref in enumerate(out_refs):

                @pl.when(place // inner == k)
                def _(ref=ref, total=total, place=place):
                    ref[place % inner] = total


def spread(where, shares, zeros):
    first = 1 + len(shares)
    return pl.pallas_call(
        functools.partial(spread_kernel, len(shares), shares[0].shape[0] // LEVELS),
        out_shape=[jax.ShapeDtypeStruct(zero.shape, zero.dtype) for zero in zeros],
        in_specs=vmem(first + len(zeros)),
        out_specs=vmem(len(zeros)),
        input_output_aliases={first + i: i for i in range(len(zeros))},
        compiler_params=pltpu.CompilerParams(vmem_limit_bytes=16 << 20),
        name="spread_terms",
    )(where, *shares, *zeros)


def merge_kernel(count, *refs):
    got_refs, out_refs = refs[:count], refs[count:]
    for i, ref in enumerate(out_refs):
        total = got_refs[0][i].astype(jnp.float32)
        for got in got_refs[1:]:
            total = total + got[i].astype(jnp.float32)
        ref[0] = total.astype(ref.dtype)


def merge(got):
    inner = got[0].shape[0]
    block = (1,) + got[0].shape[1:]
    outs = [jax.ShapeDtypeStruct(block, jnp.float32)] + [
        jax.ShapeDtypeStruct(block, jnp.bfloat16)
    ] * (inner - 1)
    return pl.pallas_call(
        functools.partial(merge_kernel, len(got)),
        out_shape=outs,
        in_specs=vmem(len(got)),
        out_specs=vmem(len(outs)),
        compiler_params=pltpu.CompilerParams(vmem_limit_bytes=16 << 20),
        name="merge_terms",
    )(*got)


def finish_kernel(keep_ref, *refs):
    out_ref = refs[-1]
    for prow, plane, row, col in pieces(*out_ref.shape[1:]):
        total = keep_ref[0, prow, plane]
        for ref in refs[:-1]:
            total = total + ref[0, prow, plane].astype(jnp.float32)
        out_ref[0, row, col] = total.astype(jnp.bfloat16)


def finish(keep, got, shape):
    return pl.pallas_call(
        finish_kernel,
        out_shape=jax.ShapeDtypeStruct(shape, jnp.bfloat16),
        in_specs=vmem(1 + len(got)),
        out_specs=vmem(1)[0],
        compiler_params=pltpu.CompilerParams(vmem_limit_bytes=4 << 20),
        name="finish_nodes",
    )(keep, *got)


def body(leaf_size, head_size, queries, leaf_latent, node_latent, grad_out, leaf_nodes, leaf_lengths):
    rows, heads, width = queries.shape
    leaves = leaf_nodes.shape[0]
    side = 1
    while side * side < leaf_size:
        side *= 2
    axes = ("leaf", "head")

    def step(value, which, distance):
        pairs = []
        for leaf in range(leaf_size):
            for head in range(head_size):
                far = (which + head) % 2 == 0
                target = leaf ^ (distance * side if far else distance)
                pairs.append((leaf * head_size + head, target * head_size + head))
        return lax.ppermute(value, axes, pairs)

    def swap(value, distance):
        return lax.ppermute(value, "head", [(i, i ^ distance) for i in range(head_size)])

    relative = leaf_nodes.reshape(1, -1) ^ lax.axis_index("leaf")
    far, near = relative // side, relative % side
    even = lax.axis_index("head") % 2 == 0
    where = jnp.where(even, near * side + far, far * side + near)

    live = jnp.arange(rows * heads // leaves, dtype=jnp.int32) // heads < leaf_lengths[:, None, None]
    live = live.astype(jnp.float32)
    order = list(range(side - 1, 0, -1))
    got = {d: step(node_latent, 0, d) for d in order}
    query = queries.reshape(rows * heads, width)
    got, query, own = lax.optimization_barrier(([got[d] for d in order], query, leaf_latent))
    inner = pack([node_latent] + got, [0] + order)
    got = {d: step(inner, 1, d) for d in order}
    table = jnp.concatenate([inner] + [got[d] for d in range(1, side)], axis=0)
    mine = select(where, table)
    parts = [swap(mine, d) for d in range(1, head_size)]
    grad = grad_out.reshape(rows * heads, LAT)
    slice_rows = node_latent.shape[1]

    expo, dprobs, *stats, near_keys = near_scores(mine, own, query, grad, leaves, heads, slice_rows)
    *terms, scale, delta, probs, keys = attend(live, query, grad, stats, parts, leaves, slice_rows)
    shares = [swap(terms[d - 1], d) for d in range(1, head_size)]
    mine, own_grad, near_probs, *zeros = own_terms(query, grad, expo, dprobs, scale, delta, mine.shape, slice_rows, rows, side)
    sends = spread(where, [mine] + shares, zeros)
    sends, probs, own_grad = lax.optimization_barrier((sends, probs, own_grad))
    got = {d: step(sends[d], 1, d) for d in order}
    attention = outputs(probs, keys, near_probs, near_keys).reshape(rows, heads, LAT)
    got, attention = lax.optimization_barrier(([sends[0]] + [got[d] for d in order], attention))
    keep, *sends = merge(got)
    got = {d: step(sends[d - 1], 0, d) for d in order}
    node_grad = finish(keep, [got[d] for d in (*range(2, side), 1)], node_latent.shape)

    leaf_grad = own_grad
    distance = 1
    while distance < head_size:
        leaf_grad = leaf_grad + swap(leaf_grad, distance)
        distance *= 2
    return (attention, node_grad, leaf_grad)


def solution(mesh):
    return jax.shard_map(
        functools.partial(body, mesh.shape["leaf"], mesh.shape["head"]),
        mesh=mesh,
        in_specs=(
            P("leaf", "head", None),
            P("leaf", None),
            P("leaf", "head", None),
            P("leaf", "head", None),
            P("leaf", None),
            P("leaf"),
        ),
        out_specs=(P("leaf", "head", None), P("leaf", "head", None), P("leaf", None)),
        check_vma=False,
    )
```

```python
import functools

import jax
import jax.numpy as jnp
from jax import lax
from jax.experimental import pallas as pl
from jax.experimental.pallas import tpu as pltpu
from jax.sharding import PartitionSpec as P

LAT = 512
LEVELS = 3

score_scale = 192.0 ** (-0.5)

NT = (((1,), (1,)), ((), ()))
NN = (((1,), (0,)), ((), ()))
TN = (((0,), (0,)), ((), ()))


def dot(a, b, dims):
    return lax.dot_general(a, b, dims, preferred_element_type=jnp.float32)


def vmem(count):
    return [pl.BlockSpec(memory_space=pltpu.VMEM)] * count


def cost(flops, moved):
    return pl.CostEstimate(flops=flops, bytes_accessed=moved, transcendentals=0)


def select_kernel(where_ref, table_ref, out_ref):
    for slot in range(out_ref.shape[0]):
        out_ref[slot] = table_ref[where_ref[0, slot]]


def select(where, table):
    slots = where.shape[1]
    shape = (slots,) + table.shape[1:]
    return pl.pallas_call(
        select_kernel,
        out_shape=jax.ShapeDtypeStruct(shape, table.dtype),
        in_specs=vmem(2),
        out_specs=vmem(1)[0],
        compiler_params=pltpu.CompilerParams(vmem_limit_bytes=4 << 20),
        name="select_nodes",
    )(where, table)


def pieces(slice_rows, width):
    lanes = 128
    full, tail = width // lanes, width % lanes
    if slice_rows % 16 or 2 * tail != lanes:
        return [(slice(0, slice_rows), slice(0, width), slice(0, slice_rows), slice(0, width))]
    out = []
    for j in range(full):
        out.append((slice(j * slice_rows, (j + 1) * slice_rows), slice(0, lanes), slice(0, slice_rows), slice(j * lanes, (j + 1) * lanes)))
    half = slice_rows // 2
    last = slice(full * slice_rows, full * slice_rows + half)
    for k in range(2):
        out.append((last, slice(k * tail, (k + 1) * tail), slice(k * half, (k + 1) * half), slice(full * lanes, width)))
    return out


def packed_shape(slice_rows, width):
    parts = pieces(slice_rows, width)
    return (max(p[0].stop for p in parts), max(p[1].stop for p in parts))


def pack_kernel(places, *refs):
    out_ref = refs[-1]
    for i, ref in zip(places, refs[:-1]):
        for prow, plane, row, col in pieces(*ref.shape[1:]):
            out_ref[i, prow, plane] = ref[0, row, col]


def pack(blocks, places):
    slice_rows, width = blocks[0].shape[1:]
    shape = (len(blocks),) + packed_shape(slice_rows, width)
    return pl.pallas_call(
        functools.partial(pack_kernel, places),
        out_shape=jax.ShapeDtypeStruct(shape, blocks[0].dtype),
        in_specs=vmem(len(blocks)),
        out_specs=vmem(1)[0],
        compiler_params=pltpu.CompilerParams(vmem_limit_bytes=4 << 20),
        name="pack_nodes",
    )(*blocks)


def store_terms(ref, first_slot, slice_rows, width, base, head_part, tail_part):
    for level in range(LEVELS):
        offset = base + level * slice_rows
        for prow, plane, row, col in pieces(slice_rows, width):
            rows = slice(offset + row.start, offset + row.stop)
            if col.start >= LAT:
                value = tail_part[rows, col.start - LAT : col.stop - LAT]
            elif col.stop <= LAT:
                value = head_part[rows, col]
            else:
                value = jnp.concatenate([head_part[rows, :], tail_part[rows, :]], axis=1)
            ref[first_slot + level, prow, plane] = value.astype(ref.dtype)


def load_keys(ref, leaf, place, part_ref, slice_rows, width):
    for level in range(LEVELS):
        offset = (place * LEVELS + level) * slice_rows
        for prow, plane, row, col in pieces(slice_rows, width):
            rows = slice(offset + row.start, offset + row.stop)
            ref[leaf, rows, col] = part_ref[leaf * LEVELS + level, prow, plane]


def near_kernel(leaves, heads, slice_rows, part_ref, own_ref, query_ref, grad_ref, expo_ref, dprob_ref, top_ref, sum_ref, dot_ref, keys_ref):
    width = own_ref.shape[1]
    leaf_rows = own_ref.shape[0] // leaves
    lines = leaf_rows * heads
    level_rows = LEVELS * slice_rows
    for leaf in range(leaves):
        load_keys(keys_ref, leaf, 0, part_ref, slice_rows, width)
        keys_ref[leaf, level_rows:, :] = own_ref[leaf * leaf_rows : (leaf + 1) * leaf_rows, :]
        query = query_ref[leaf * lines : (leaf + 1) * lines, :]
        grad = grad_ref[leaf * lines : (leaf + 1) * lines, :]
        scores = dot(keys_ref[leaf], query, NT) * score_scale
        row_of = lax.broadcasted_iota(jnp.int32, (leaf_rows, lines), 1) // heads
        own_key = lax.broadcasted_iota(jnp.int32, (leaf_rows, lines), 0)
        own_scores = jnp.where(own_key <= row_of, scores[level_rows:], -jnp.inf)
        scores = jnp.concatenate([scores[:level_rows], own_scores], axis=0)
        top = jnp.max(scores, axis=0, keepdims=True)
        expo = jnp.exp(scores - top)
        dprobs = dot(keys_ref[leaf, :, :LAT], grad, NT)
        expo_ref[leaf] = expo
        dprob_ref[leaf] = dprobs
        top_ref[leaf] = top
        sum_ref[leaf] = jnp.sum(expo, axis=0, keepdims=True)
        dot_ref[leaf] = jnp.sum(expo * dprobs, axis=0, keepdims=True)


def near_scores(part, own, query, grad, leaves, heads, slice_rows):
    rows, width = own.shape
    lines = rows * heads // leaves
    near_rows = LEVELS * slice_rows + rows // leaves
    line = jax.ShapeDtypeStruct((leaves, 1, lines), jnp.float32)
    outs = [
        jax.ShapeDtypeStruct((leaves, near_rows, lines), jnp.float32),
        jax.ShapeDtypeStruct((leaves, near_rows, lines), jnp.float32),
        line,
        line,
        line,
        jax.ShapeDtypeStruct((leaves, near_rows, width), jnp.bfloat16),
    ]
    return pl.pallas_call(
        functools.partial(near_kernel, leaves, heads, slice_rows),
        out_shape=outs,
        in_specs=vmem(4),
        out_specs=vmem(len(outs)),
        compiler_params=pltpu.CompilerParams(vmem_limit_bytes=24 << 20),
        cost_estimate=cost(2 * rows * heads * near_rows * 2 * width, 4 << 20),
        name="near_scores",
    )(part, own, query, grad)


def attend_kernel(parts, leaves, slice_rows, live_ref, query_ref, grad_ref, top_ref, sum_ref, dot_ref, *refs):
    part_refs, refs = refs[:parts], refs[parts:]
    term_refs, refs = refs[:parts], refs[parts:]
    near_scale_ref, delta_ref, probs_ref, keys_ref, dscores_ref = refs
    width = query_ref.shape[1]
    lines = query_ref.shape[0] // leaves
    level_rows = LEVELS * slice_rows
    for leaf in range(leaves):
        query = query_ref[leaf * lines : (leaf + 1) * lines, :]
        grad = grad_ref[leaf * lines : (leaf + 1) * lines, :]
        for place in range(parts):
            load_keys(keys_ref, leaf, place, part_refs[place], slice_rows, width)
        scores = dot(keys_ref[leaf], query, NT) * score_scale
        dprobs = dot(keys_ref[leaf, :, :LAT], grad, NT)
        top = jnp.maximum(top_ref[leaf], jnp.max(scores, axis=0, keepdims=True))
        shift = jnp.exp(top_ref[leaf] - top)
        expo = jnp.exp(scores - top)
        total = shift * sum_ref[leaf] + jnp.sum(expo, axis=0, keepdims=True)
        scale = live_ref[leaf] / total
        delta = (shift * dot_ref[leaf] + jnp.sum(expo * dprobs, axis=0, keepdims=True)) * scale
        near_scale_ref[leaf] = shift * scale
        delta_ref[leaf] = delta
        probs = expo * scale
        probs_ref[leaf] = probs.astype(jnp.bfloat16)
        dscores_ref[...] = (score_scale * probs * (dprobs - delta)).astype(jnp.bfloat16)
        head_part, tail_part = key_grads(dscores_ref[...], probs_ref[leaf], query, grad)
        for place in range(parts):
            store_terms(term_refs[place], leaf * LEVELS, slice_rows, width, place * level_rows, head_part, tail_part)


def key_grads(dscores, probs_b, query, grad):
    head_part = dot(dscores, query[:, :LAT], NN) + dot(probs_b, grad, NN)
    return head_part, dot(dscores, query[:, LAT:], NN)


def attend(live, query, grad, stats, parts, leaves, slice_rows):
    width = query.shape[1]
    lines = live.shape[2]
    sent_rows = LEVELS * len(parts) * slice_rows
    line = jax.ShapeDtypeStruct((leaves, 1, lines), jnp.float32)
    outs = [jax.ShapeDtypeStruct(part.shape, jnp.bfloat16) for part in parts] + [
        line,
        line,
        jax.ShapeDtypeStruct((leaves, sent_rows, lines), jnp.bfloat16),
        jax.ShapeDtypeStruct((leaves, sent_rows, width), jnp.bfloat16),
    ]
    return pl.pallas_call(
        functools.partial(attend_kernel, len(parts), leaves, slice_rows),
        out_shape=outs,
        in_specs=vmem(6 + len(parts)),
        out_specs=vmem(len(outs)),
        scratch_shapes=[pltpu.VMEM((sent_rows, lines), jnp.bfloat16)],
        compiler_params=pltpu.CompilerParams(vmem_limit_bytes=40 << 20),
        cost_estimate=cost(2 * leaves * lines * sent_rows * 4 * width, 8 << 20),
        name="attend",
    )(live, query, grad, *stats, *parts)


def own_kernel(leaves, slice_rows, query_ref, grad_ref, expo_ref, dprob_ref, scale_ref, delta_ref, term_ref, own_grad_ref, probs_ref, *refs):
    dscores_ref = refs[-1]
    for ref in refs[:-1]:
        ref[...] = jnp.zeros_like(ref)
    lines = query_ref.shape[0] // leaves
    width = query_ref.shape[1]
    leaf_rows = own_grad_ref.shape[0] // leaves
    level_rows = LEVELS * slice_rows
    for leaf in range(leaves):
        query = query_ref[leaf * lines : (leaf + 1) * lines, :]
        grad = grad_ref[leaf * lines : (leaf + 1) * lines, :]
        probs = expo_ref[leaf] * scale_ref[leaf]
        probs_ref[leaf] = probs.astype(jnp.bfloat16)
        dscores_ref[...] = (score_scale * probs * (dprob_ref[leaf] - delta_ref[leaf])).astype(jnp.bfloat16)
        head_part, tail_part = key_grads(dscores_ref[...], probs_ref[leaf], query, grad)
        store_terms(term_ref, leaf * LEVELS, slice_rows, width, 0, head_part, tail_part)
        rows = slice(leaf * leaf_rows, (leaf + 1) * leaf_rows)
        own_grad_ref[rows, :LAT] = head_part[level_rows:].astype(jnp.bfloat16)
        own_grad_ref[rows, LAT:] = tail_part[level_rows:].astype(jnp.bfloat16)


def own_terms(query, grad, expo, dprobs, scale, delta, block, slice_rows, rows, side):
    leaves, near_rows, lines = expo.shape
    width = query.shape[1]
    outs = [
        jax.ShapeDtypeStruct(block, jnp.float32),
        jax.ShapeDtypeStruct((rows, width), jnp.bfloat16),
        jax.ShapeDtypeStruct(expo.shape, jnp.bfloat16),
    ] + [jax.ShapeDtypeStruct((side,) + block[1:], jnp.bfloat16)] * side
    return pl.pallas_call(
        functools.partial(own_kernel, leaves, slice_rows),
        out_shape=outs,
        in_specs=vmem(6),
        out_specs=vmem(len(outs)),
        scratch_shapes=[pltpu.VMEM((near_rows, lines), jnp.bfloat16)],
        compiler_params=pltpu.CompilerParams(vmem_limit_bytes=24 << 20),
        cost_estimate=cost(2 * leaves * lines * near_rows * 2 * width, 4 << 20),
        name="own_terms",
    )(query, grad, expo, dprobs, scale, delta)


def outputs_kernel(leaves, probs_ref, keys_ref, near_probs_ref, near_keys_ref, out_ref):
    lines = probs_ref.shape[2]
    for leaf in range(leaves):
        out = dot(probs_ref[leaf], keys_ref[leaf, :, :LAT], TN)
        out = out + dot(near_probs_ref[leaf], near_keys_ref[leaf, :, :LAT], TN)
        out_ref[leaf * lines : (leaf + 1) * lines, :] = out.astype(jnp.bfloat16)


def outputs(probs, keys, near_probs, near_keys):
    leaves, sent_rows, lines = probs.shape
    total_keys = sent_rows + near_probs.shape[1]
    return pl.pallas_call(
        functools.partial(outputs_kernel, leaves),
        out_shape=jax.ShapeDtypeStruct((leaves * lines, LAT), jnp.bfloat16),
        in_specs=vmem(4),
        out_specs=vmem(1)[0],
        compiler_params=pltpu.CompilerParams(vmem_limit_bytes=24 << 20),
        cost_estimate=cost(2 * leaves * total_keys * lines * LAT, 4 << 20),
        name="attend_outputs",
    )(probs, keys, near_probs, near_keys)


def spread_kernel(shares, leaves, where_ref, *refs):
    share_refs, refs = refs[:shares], refs[shares:]
    out_refs = refs[len(refs) // 2 :]
    inner = out_refs[0].shape[0]
    for level in range(LEVELS):
        slots = [leaf * LEVELS + level for leaf in range(leaves)]
        places = {slot: where_ref[0, slot] for slot in slots}
        totals = []
        for slot in slots:
            total = share_refs[0][slot]
            for ref in share_refs[1:]:
                total = total + ref[slot].astype(jnp.float32)
            totals.append(total)
        for i, slot in enumerate(slots):
            total = totals[i]
            for j, other in enumerate(slots):
                if j != i:
                    shared = places[other] == places[slot]
                    total = total + jnp.where(shared, totals[j], 0.0)
            total = total.astype(jnp.bfloat16)
            place = places[slot]
            for k, ref in enumerate(out_refs):

                @pl.when(place // inner == k)
                def _(ref=ref, total=total, place=place):
                    ref[place % inner] = total


def spread(where, shares, zeros):
    first = 1 + len(shares)
    return pl.pallas_call(
        functools.partial(spread_kernel, len(shares), shares[0].shape[0] // LEVELS),
        out_shape=[jax.ShapeDtypeStruct(zero.shape, zero.dtype) for zero in zeros],
        in_specs=vmem(first + len(zeros)),
        out_specs=vmem(len(zeros)),
        input_output_aliases={first + i: i for i in range(len(zeros))},
        compiler_params=pltpu.CompilerParams(vmem_limit_bytes=16 << 20),
        name="spread_terms",
    )(where, *shares, *zeros)


def merge_kernel(count, *refs):
    got_refs, out_refs = refs[:count], refs[count:]
    for i, ref in enumerate(out_refs):
        total = got_refs[0][i].astype(jnp.float32)
        for got in got_refs[1:]:
            total = total + got[i].astype(jnp.float32)
        ref[0] = total.astype(ref.dtype)


def merge(got):
    inner = got[0].shape[0]
    block = (1,) + got[0].shape[1:]
    outs = [jax.ShapeDtypeStruct(block, jnp.float32)] + [
        jax.ShapeDtypeStruct(block, jnp.bfloat16)
    ] * (inner - 1)
    return pl.pallas_call(
        functools.partial(merge_kernel, len(got)),
        out_shape=outs,
        in_specs=vmem(len(got)),
        out_specs=vmem(len(outs)),
        compiler_params=pltpu.CompilerParams(vmem_limit_bytes=16 << 20),
        name="merge_terms",
    )(*got)


def finish_kernel(keep_ref, *refs):
    out_ref = refs[-1]
    for prow, plane, row, col in pieces(*out_ref.shape[1:]):
        total = keep_ref[0, prow, plane]
        for ref in refs[:-1]:
            total = total + ref[0, prow, plane].astype(jnp.float32)
        out_ref[0, row, col] = total.astype(jnp.bfloat16)


def finish(keep, got, shape):
    return pl.pallas_call(
        finish_kernel,
        out_shape=jax.ShapeDtypeStruct(shape, jnp.bfloat16),
        in_specs=vmem(1 + len(got)),
        out_specs=vmem(1)[0],
        compiler_params=pltpu.CompilerParams(vmem_limit_bytes=4 << 20),
        name="finish_nodes",
    )(keep, *got)


def body(leaf_size, head_size, queries, leaf_latent, node_latent, grad_out, leaf_nodes, leaf_lengths):
    rows, heads, width = queries.shape
    leaves = leaf_nodes.shape[0]
    side = 1
    while side * side < leaf_size:
        side *= 2
    axes = ("leaf", "head")

    def step(value, which, distance):
        pairs = []
        for leaf in range(leaf_size):
            for head in range(head_size):
                far = (which + head) % 2 == 0
                target = leaf ^ (distance * side if far else distance)
                pairs.append((leaf * head_size + head, target * head_size + head))
        return lax.ppermute(value, axes, pairs)

    def swap(value, distance):
        return lax.ppermute(value, "head", [(i, i ^ distance) for i in range(head_size)])

    relative = leaf_nodes.reshape(1, -1) ^ lax.axis_index("leaf")
    far, near = relative // side, relative % side
    even = lax.axis_index("head") % 2 == 0
    where = jnp.where(even, near * side + far, far * side + near)

    live = jnp.arange(rows * heads // leaves, dtype=jnp.int32) // heads < leaf_lengths[:, None, None]
    live = live.astype(jnp.float32)
    order = list(range(side - 1, 0, -1))
    got = {d: step(node_latent, 0, d) for d in order}
    query = queries.reshape(rows * heads, width)
    got, query, own = lax.optimization_barrier(([got[d] for d in order], query, leaf_latent))
    inner = pack([node_latent] + got, [0] + order)
    got = {d: step(inner, 1, d) for d in order}
    line_up = sorted(range(1, side), key=lambda d: (d == side - 1, d == 1))
    outer = where // side
    spot = sum([jnp.where(outer == d, i + 1, 0) for i, d in enumerate(line_up)])
    table = jnp.concatenate([inner] + [got[d] for d in line_up], axis=0)
    mine = select(spot * side + where % side, table)
    parts = [swap(mine, d) for d in range(1, head_size)]
    grad = grad_out.reshape(rows * heads, LAT)
    slice_rows = node_latent.shape[1]

    expo, dprobs, *stats, near_keys = near_scores(mine, own, query, grad, leaves, heads, slice_rows)
    *terms, scale, delta, probs, keys = attend(live, query, grad, stats, parts, leaves, slice_rows)
    shares = [swap(terms[d - 1], d) for d in range(1, head_size)]
    mine, own_grad, near_probs, *zeros = own_terms(query, grad, expo, dprobs, scale, delta, mine.shape, slice_rows, rows, side)
    sends = spread(where, [mine] + shares, zeros)
    sends, probs, own_grad = lax.optimization_barrier((sends, probs, own_grad))
    got = {d: step(sends[d], 1, d) for d in order}
    attention = outputs(probs, keys, near_probs, near_keys).reshape(rows, heads, LAT)
    got, attention = lax.optimization_barrier(([sends[0]] + [got[d] for d in sorted(range(1, side), key=lambda d: (d != side - 1, d != 1))], attention))
    keep, *sends = merge(got)
    got = {d: step(sends[d - 1], 0, d) for d in order}
    node_grad = finish(keep, [got[d] for d in (*range(2, side), 1)], node_latent.shape)

    leaf_grad = own_grad
    distance = 1
    while distance < head_size:
        leaf_grad = leaf_grad + swap(leaf_grad, distance)
        distance *= 2
    return (attention, node_grad, leaf_grad)


def solution(mesh):
    return jax.shard_map(
        functools.partial(body, mesh.shape["leaf"], mesh.shape["head"]),
        mesh=mesh,
        in_specs=(
            P("leaf", "head", None),
            P("leaf", None),
            P("leaf", "head", None),
            P("leaf", "head", None),
            P("leaf", None),
            P("leaf"),
        ),
        out_specs=(P("leaf", "head", None), P("leaf", "head", None), P("leaf", None)),
        check_vma=False,
    )
```
